32 devices in a mesh: occ: 8 (over y, x, core), vir: 4 (over z).
Axes of the slice: x: 2, y: 2, z: 4, core: 2. Of those that a mesh axis runs over, the one named last changes fastest.
Arguments:
- ints_alpha: bfloat16 [1536, 8, 1024], P('occ', None, 'vir'), may hold values from -0.71875 to 0.71875
- ints_beta: bfloat16 [1536, 8, 1024], P('occ', None, 'vir'), may hold values from -0.71875 to 0.71875
- metric: bfloat16 [1536, 1536], P('vir'), may hold values from -0.5 to 1.5, as said below
- e_occ_alpha: float32 [8], P('occ'), may hold values from -2 to -0.3
- e_occ_beta: float32 [8], replicated, may hold values from -2 to -0.3
- e_vir_alpha: float32 [1024], replicated, may hold values from 0.2 to 3
- e_vir_beta: float32 [1024], P('vir'), may hold values from 0.2 to 3
Outputs:
- gamma_alpha: bfloat16 [1536, 8, 1024], P(None, 'occ', 'vir')
- gamma_beta: bfloat16 [1536, 8, 1024], P(None, 'occ', 'vir')
The draws below stay inside these ranges and needn't reach their ends.
Inputs may be any that keep to these rules, and one draw needn't show every extreme that they name: `metric`: symmetric and positive definite.
All inputs are finite; a program needn't handle non-finite values.
Results may differ from the reference program's by a relative error of at most 0.009.
Values may be sent and summed in bfloat16 or wider, within the bound.
No kernel may reach another device: no remote copies, remote signals or barrier semaphores. Data moves between devices by JAX's collectives and lax.ppermute only.
A program may use at most 64 MiB of HBM per device.

```python
import math
import jax
import jax.numpy as jnp
from jax import lax

NAUX = 1536
NVIR = 1024
OCC_DEV = 1
PAIR_STEPS = 2
NOCC = 8
N_OCC = 8
N_VIR = 4


def draw_metric(key, part):
    gaussian = jax.random.normal(jax.random.fold_in(key, 17), (NAUX, NAUX), jnp.float32)
    strength = 0.3
    symmetric = (gaussian + gaussian.T) * (strength / math.sqrt(2.0 * NAUX))
    return (jnp.eye(NAUX, dtype=jnp.float32) + symmetric).astype(jnp.bfloat16)


def levels(key, extent, split, low, high):
    loudness, own = 1.0, jax.random.fold_in(key, 6)
    for axis_at, shards_of in split:
        heights = jnp.exp(jax.random.uniform(jax.random.fold_in(own, axis_at), (shards_of,), jnp.float32, low / len(split), high / len(split)))
        loudness = loudness * jnp.repeat(heights, extent[axis_at] // shards_of).reshape([-1 if axis == axis_at else 1 for axis in range(len(extent))])
    return loudness


def centred(key, shape, scale, bound, cuts=(), kind=jnp.bfloat16):
    array = jax.random.normal(key, shape, jnp.float32) * scale
    if len(cuts) > 0:
        array = levels(key, shape, cuts, -0.22, 0.18) * array
    return jnp.clip(array, min=-bound, max=bound).astype(kind)


def setup_inputs(seed: int = 0) -> dict:
    seeds = jax.random.split(jax.random.key(seed), 8)
    return {
        "ints_alpha": centred(seeds[0], (NAUX, NOCC, NVIR), 0.12, 0.71875, ((0, 8), (2, 4))),
        "ints_beta": centred(seeds[1], (NAUX, NOCC, NVIR), 0.12, 0.71875, ((0, 8), (2, 4))),
        "metric": draw_metric(jax.random.fold_in(seeds[7], 71), 0),
        "e_occ_alpha": jnp.clip(-2.0 + 1.7 * jax.random.uniform(seeds[3], (NOCC,), jnp.float32) ** levels(seeds[3], (NOCC,), ((0, 8),), -0.2, 0.2), -2.0, -0.3),
        "e_occ_beta": jnp.clip(jax.random.uniform(seeds[4], (NOCC,), jnp.float32, -2.0, -0.3), -2.0, -0.3),
        "e_vir_alpha": jnp.clip(jax.random.uniform(seeds[5], (NVIR,), jnp.float32, 0.2, 3.0), 0.2, 3.0),
        "e_vir_beta": jnp.clip(0.2 + 2.8 * jax.random.uniform(seeds[6], (NVIR,), jnp.float32) ** levels(seeds[6], (NVIR,), ((0, 4),), -0.2, 0.2), 0.2, 3.0),
    }


def transform(metric, raw_ints):
    flat = raw_ints.reshape(NAUX, NOCC * NVIR)
    fitted = jnp.dot(metric, flat, preferred_element_type=jnp.float32).astype(jnp.bfloat16)
    return fitted.reshape(NAUX, N_OCC, OCC_DEV * NVIR).transpose(1, 0, 2)


def reference(ints_alpha, ints_beta, metric, e_occ_alpha, e_occ_beta, e_vir_alpha, e_vir_beta):
    fitted_alpha = transform(metric, ints_alpha)
    fitted_beta = transform(metric, ints_beta)
    left_energy = (e_occ_alpha.reshape(N_OCC, OCC_DEV, 1) - e_vir_alpha[None, None, :]).reshape(N_OCC, OCC_DEV * NVIR)
    right_energy = (e_occ_beta.reshape(N_OCC, OCC_DEV, 1) - e_vir_beta[None, None, :]).reshape(N_OCC, OCC_DEV * NVIR)
    block_ids = jnp.arange(N_OCC, dtype=jnp.int32)
    vir_slice = NVIR // N_VIR

    def block_terms(block_index):
        alpha_block = fitted_alpha[block_index]
        slice_total = jnp.zeros((N_VIR, NAUX, OCC_DEV * NVIR), jnp.float32)
        beta_list = []
        for hop_bit in range(PAIR_STEPS):
            partner = jnp.bitwise_xor(block_index, 1 << hop_bit).astype(jnp.int32)
            beta_block = fitted_beta[partner]
            pair_ints = lax.dot_general(alpha_block, beta_block, (((0,), (0,)), ((), ())), preferred_element_type=jnp.float32)
            denominator = left_energy[block_index][:, None] + right_energy[partner][None, :]
            amplitude = (pair_ints / denominator).astype(jnp.bfloat16)
            beta_split = beta_block.astype(jnp.float32).reshape(NAUX, OCC_DEV, N_VIR, vir_slice)
            amp_split = amplitude.astype(jnp.float32).reshape(OCC_DEV * NVIR, OCC_DEV, N_VIR, vir_slice)
            slice_total = slice_total + jnp.einsum("posv,xosv->spx", beta_split, amp_split)
            beta_list.append(jnp.dot(alpha_block, amplitude, preferred_element_type=jnp.float32))
        rounded = lax.optimization_barrier(slice_total.astype(jnp.bfloat16))
        alpha_sum = jnp.sum(rounded.astype(jnp.float32), axis=0)
        return alpha_sum, jnp.stack(beta_list)

    alpha_total, beta_terms = lax.map(block_terms, block_ids)
    beta_total = jnp.zeros((N_OCC, NAUX, OCC_DEV * NVIR), jnp.float32)
    for hop_bit in range(PAIR_STEPS):
        partner_ids = jnp.bitwise_xor(block_ids, 1 << hop_bit).astype(jnp.int32)
        beta_total = beta_total + beta_terms[partner_ids, hop_bit]

    def unfold(total):
        shaped = total.reshape(N_OCC, NAUX, OCC_DEV, NVIR).transpose(1, 0, 2, 3)
        return shaped.reshape(NAUX, NOCC, NVIR).astype(jnp.bfloat16)

    return unfold(alpha_total), unfold(beta_total)
```

```python
import jax
import jax.numpy as jnp
from jax import lax
from jax.sharding import PartitionSpec as P

PAIR_STEPS = 2
BF16, F32 = jnp.bfloat16, jnp.float32


def swap(value, axis, mask):
    pairs = [(source, source ^ mask) for source in range(lax.axis_size(axis))]
    return lax.ppermute(value, axis, pairs)


def alpha_of(device):
    return device ^ (2 * (device & 1))


def beta_of(device):
    return device ^ (2 * (1 - (device & 1)))


def absolute(pieces, shift):
    return [lax.select_n(shift ^ k, *pieces) for k in range(len(pieces))]


def regroup(ints_alpha, ints_beta, occ_dev):
    blocks = lax.axis_size("occ")
    chips = blocks // 2
    rows, _, cols = ints_alpha.shape
    cut = lambda a, k: a[:, k * occ_dev : (k + 1) * occ_dev].reshape(rows, occ_dev * cols)
    table = jnp.stack(
        [
            jnp.stack([cut(ints_alpha, alpha_of(d)), cut(ints_beta, beta_of(d))])
            for d in range(blocks)
        ]
    )
    if chips > 4:
        got = lax.all_to_all(table, "occ", split_axis=0, concat_axis=0, tiled=True)
        got = jnp.moveaxis(got, 1, 0).reshape(2, blocks * rows, occ_dev * cols)
        return got[0], got[1]
    table = table.reshape(chips, 2, 2, rows, occ_dev * cols)
    me = lax.axis_index("occ")
    chip, core = me // 2, me % 2
    held = []
    for m in range(chips):
        part = lax.dynamic_index_in_dim(table, chip ^ m, 0, keepdims=False)
        held.append(part if m == 0 else swap(part, "occ", 2 * m))
    keep = [lax.dynamic_index_in_dim(h, core, 0, keepdims=False) for h in held]
    give = jnp.stack([lax.dynamic_index_in_dim(h, 1 - core, 0, keepdims=False) for h in held])
    take = swap(give, "occ", 1)
    order = []
    for m in range(chips):
        own, other = keep[m], take[m]
        lo = jnp.where(core == 0, own, other)
        hi = jnp.where(core == 0, other, own)
        order.append(jnp.concatenate([lo, hi], axis=1))
    full = jnp.concatenate(absolute(order, chip), axis=1)
    return full[0], full[1]


def whole_metric(metric):
    rows = metric.shape[0]
    half = rows // 2
    core, layer = lax.axis_index("occ") % 2, lax.axis_index("vir")
    mine = lax.dynamic_slice_in_dim(metric, core * half, half, 0)
    one, three = swap(mine, "vir", 1), swap(mine, "vir", 3)
    two = jnp.concatenate(
        [swap(three[: half // 2], "vir", 1), swap(one[half // 2 :], "vir", 3)], axis=0
    )
    got = jnp.stack([one, two, three])
    other = swap(got, "occ", 1)
    lo = jnp.where(core == 0, got, other)
    hi = jnp.where(core == 0, other, got)
    rest = jnp.concatenate([lo, hi], axis=1)
    pieces = [metric, rest[0], rest[1], rest[2]]
    return jnp.concatenate(absolute(pieces, layer), axis=0)


def dots(a, b, da, db):
    return lax.dot_general(a, b, (((da,), (db,)), ((), ())), preferred_element_type=F32)


def ring(ints_alpha, ints_beta, metric, e_occ_alpha, e_occ_beta, e_vir_alpha, e_vir_beta):
    aux = metric.shape[1]
    occ_dev = e_occ_alpha.shape[0]
    vir = e_vir_beta.shape[0]
    unit = occ_dev * vir
    blocks = lax.axis_size("occ")
    me, layer = lax.axis_index("occ"), lax.axis_index("vir")
    core = me % 2

    raw_alpha, raw_beta = regroup(ints_alpha, ints_beta, occ_dev)
    near_alpha, near_beta = swap(raw_alpha, "vir", 1), swap(raw_beta, "vir", 3)
    square = whole_metric(metric)
    raw = jnp.concatenate([raw_alpha, near_alpha, raw_beta, near_beta], axis=1)
    fitted = dots(square, raw, 1, 0).astype(BF16)
    mine, beta = fitted[:, : 2 * unit], fitted[:, 2 * unit :]
    alpha = jnp.concatenate([mine, swap(mine, "occ", 1)], axis=1)

    occ_mine = lax.ppermute(e_occ_alpha, "occ", [(alpha_of(d), d) for d in range(blocks)])
    occ_other = swap(occ_mine, "occ", 1)
    cut = lambda k: lax.dynamic_slice_in_dim(e_vir_alpha, k * vir, vir)
    vir_alpha = [cut(layer), cut(layer ^ 1)]
    left = jnp.concatenate(
        [(o[:, None] - v[None, :]).reshape(-1) for o in (occ_mine, occ_other) for v in vir_alpha]
    )
    occ_right = lax.dynamic_slice_in_dim(e_occ_beta, beta_of(me) * occ_dev, occ_dev)
    vir_beta = [e_vir_beta, swap(e_vir_beta, "vir", 3)]
    right = jnp.concatenate([(occ_right[:, None] - v[None, :]).reshape(-1) for v in vir_beta])

    pair_ints = dots(alpha, beta, 0, 0)
    amplitude = (pair_ints / (left[:, None] + right[None, :])).astype(BF16)

    gamma_beta = dots(alpha, amplitude, 1, 0)
    gamma_alpha = dots(beta, amplitude, 1, 1)
    from_core = swap(gamma_alpha[:, 2 * unit :].astype(BF16), "occ", 1)
    gamma_alpha = gamma_alpha[:, : 2 * unit] + from_core.astype(F32)
    from_one = swap(gamma_alpha[:, unit:].astype(BF16), "vir", 1)
    from_three = swap(gamma_beta[:, unit:].astype(BF16), "vir", 3)
    done_alpha = (gamma_alpha[:, :unit] + from_one.astype(F32)).astype(BF16)
    done_beta = (gamma_beta[:, :unit] + from_three.astype(F32)).astype(BF16)
    moved = swap(jnp.where(core == 1, done_alpha, done_beta), "occ", 2)
    out_alpha = jnp.where(core == 1, moved, done_alpha)
    out_beta = jnp.where(core == 1, done_beta, moved)
    shape = (aux, occ_dev, vir)
    return out_alpha.reshape(shape), out_beta.reshape(shape)


def solution(mesh):
    in_specs = (
        P("occ", None, "vir"),
        P("occ", None, "vir"),
        P("vir", None),
        P("occ"),
        P(),
        P(),
        P("vir"),
    )
    out_specs = (P(None, "occ", "vir"), P(None, "occ", "vir"))
    return jax.shard_map(ring, mesh=mesh, in_specs=in_specs, out_specs=out_specs, check_vma=False)
```

```python
import jax
import jax.numpy as jnp
from jax import lax
from jax.experimental import pallas as pl
from jax.experimental.pallas import tpu as pltpu
from jax.sharding import PartitionSpec as P

PAIR_STEPS = 2
BF16, F32 = jnp.bfloat16, jnp.float32
VMEM = pl.BlockSpec(memory_space=pltpu.VMEM)


def swap(value, axis, mask):
    pairs = [(source, source ^ mask) for source in range(lax.axis_size(axis))]
    return lax.ppermute(value, axis, pairs)


def alpha_of(device):
    return device ^ (2 * (device & 1))


def beta_of(device):
    return device ^ (2 * (1 - (device & 1)))


def local_call(kernel, shapes, *args):
    return pl.pallas_call(
        kernel,
        out_shape=shapes,
        in_specs=[VMEM] * len(args),
        out_specs=jax.tree.map(lambda _: VMEM, shapes),
        cost_estimate=pl.CostEstimate(flops=0, bytes_accessed=4 << 20, transcendentals=0),
        compiler_params=pltpu.CompilerParams(vmem_limit_bytes=32 << 20),
    )(*args)


def place_rows(chips, *refs):
    held, take, out = refs[:chips], refs[chips], refs[-1]
    rows = take.shape[1]
    me = lax.axis_index("occ")
    chip, core = me // 2, me % 2
    for m in range(chips):
        at = 2 * (chip ^ m) * rows
        out[pl.ds(pl.multiple_of(at + core * rows, rows), rows), :] = held[m][core]
        out[pl.ds(pl.multiple_of(at + (1 - core) * rows, rows), rows), :] = take[m]


def regroup(ints, index_of, occ_dev):
    blocks = lax.axis_size("occ")
    chips = blocks // 2
    rows, _, cols = ints.shape
    unit = occ_dev * cols
    table = ints.reshape(rows, blocks, unit).transpose(1, 0, 2)
    me = lax.axis_index("occ")
    chip, core = me // 2, me % 2
    if chips > 4:
        table = jnp.stack([table[index_of(d)] for d in range(blocks)])
        got = lax.all_to_all(table, "occ", split_axis=0, concat_axis=0, tiled=True)
        return got.reshape(blocks * rows, unit)
    held = []
    for m in range(chips):
        first = 2 * (chip ^ m)
        part = jnp.stack(
            [lax.dynamic_index_in_dim(table, index_of(first + c), 0, keepdims=False) for c in (0, 1)]
        )
        held.append(part if m == 0 else swap(part, "occ", 2 * m))
    give = jnp.stack([lax.dynamic_index_in_dim(h, 1 - core, 0, keepdims=False) for h in held])
    take = swap(give, "occ", 1)
    shape = jax.ShapeDtypeStruct((blocks * rows, unit), BF16)
    return local_call(lambda *refs: place_rows(chips, *refs), shape, *held, take)


def halves_metric(metric):
    rows = metric.shape[0]
    half = rows // 2
    core, layer = lax.axis_index("occ") % 2, lax.axis_index("vir")
    mine = lax.dynamic_slice_in_dim(metric, core * half, half, 0)
    got = jnp.stack([swap(mine, "vir", k) for k in (1, 2, 3)])
    other = swap(got, "occ", 1)
    lo, hi = jnp.where(core == 0, got, other), jnp.where(core == 0, other, got)
    rest = jnp.concatenate([lo, hi], axis=1)
    pieces = [metric, rest[0], rest[1], rest[2]]
    return jnp.concatenate([lax.select_n(layer ^ k, *pieces) for k in range(4)], axis=0)


def place_metric(chips, *refs):
    own, mine, other, out = refs[0], refs[1 : 1 + chips], refs[1 + chips : 1 + 2 * chips], refs[-1]
    rows = own.shape[0]
    part = mine[0].shape[1]
    me, layer = lax.axis_index("occ"), lax.axis_index("vir")
    chip, core = me // 2, me % 2
    out[pl.ds(pl.multiple_of(layer * rows, rows), rows), :] = own[...]
    for k in (1, 2, 3):
        for m in range(chips):
            for c, held in ((core, mine), (1 - core, other)):
                at = (layer ^ k) * rows + (2 * (chip ^ m) + c) * part
                out[pl.ds(pl.multiple_of(at, part), part), :] = held[m][k - 1]


def whole_metric(metric):
    rows = metric.shape[0]
    blocks = lax.axis_size("occ")
    chips = blocks // 2
    if chips > 4 or rows % (16 * blocks):
        return halves_metric(metric)
    part = rows // blocks
    mine = lax.dynamic_slice_in_dim(metric, lax.axis_index("occ") * part, part, 0)
    got = jnp.stack([swap(mine, "vir", k) for k in (1, 2, 3)])
    plane = [got] + [swap(got, "occ", 2 * m) for m in range(1, chips)]
    other = [swap(p, "occ", 1) for p in plane]
    shape = jax.ShapeDtypeStruct((metric.shape[1], metric.shape[1]), BF16)
    return local_call(lambda *refs: place_metric(chips, *refs), shape, metric, *plane, *other)


def dots(a, b, da, db):
    return lax.dot_general(a, b, (((da,), (db,)), ((), ())), preferred_element_type=F32)


def ring(ints_alpha, ints_beta, metric, e_occ_alpha, e_occ_beta, e_vir_alpha, e_vir_beta):
    aux = metric.shape[1]
    occ_dev = e_occ_alpha.shape[0]
    vir = e_vir_beta.shape[0]
    unit = occ_dev * vir
    blocks, layers = lax.axis_size("occ"), lax.axis_size("vir")
    me, layer = lax.axis_index("occ"), lax.axis_index("vir")
    core = me % 2

    square = whole_metric(metric)
    raw_beta = regroup(ints_beta, beta_of, occ_dev)
    raw_alpha = regroup(ints_alpha, alpha_of, occ_dev)

    occ_mine = lax.ppermute(e_occ_alpha, "occ", [(alpha_of(d), d) for d in range(blocks)])
    occ_other = swap(occ_mine, "occ", 1)
    cut = lambda k: lax.dynamic_slice_in_dim(e_vir_alpha, k * vir, vir)
    vir_alpha = [cut(layer), cut(layer ^ 1)]
    left = jnp.concatenate(
        [(o[:, None] - v[None, :]).reshape(-1) for o in (occ_mine, occ_other) for v in vir_alpha]
    )
    occ_right = lax.dynamic_slice_in_dim(e_occ_beta, beta_of(me) * occ_dev, occ_dev)
    vir_beta = [e_vir_beta, swap(e_vir_beta, "vir", 3)]
    right = jnp.concatenate([(occ_right[:, None] - v[None, :]).reshape(-1) for v in vir_beta])

    near_beta = swap(raw_beta, "vir", 3)
    near_alpha = swap(raw_alpha, "vir", 1)
    fit = lambda *raw: dots(square, jnp.concatenate(raw, axis=1), 1, 0).astype(BF16)
    own = fit(raw_alpha, raw_beta)
    near = fit(near_alpha, near_beta)
    mine = jnp.concatenate([own[:, :unit], near[:, :unit]], axis=1)
    beta = jnp.concatenate([own[:, unit:], near[:, unit:]], axis=1)
    alpha = jnp.concatenate([mine, swap(mine, "occ", 1)], axis=1)

    pair_ints = dots(alpha, beta, 0, 0)
    amplitude = (pair_ints / (left[:, None] + right[None, :])).astype(BF16)

    gamma_alpha = dots(beta, amplitude, 1, 1)
    from_core = swap(gamma_alpha[:, 2 * unit :].astype(BF16), "occ", 1)
    gamma_beta = dots(alpha, amplitude, 1, 0)
    gamma_alpha = gamma_alpha[:, : 2 * unit] + from_core.astype(F32)
    first = jnp.where(core == 1, gamma_alpha, gamma_beta)
    second = jnp.where(core == 1, gamma_beta, gamma_alpha)

    def back(value, odd, even):
        pairs = [
            (d * layers + v, d * layers + (v ^ (odd if d % 2 else even)))
            for d in range(blocks)
            for v in range(layers)
        ]
        got = lax.ppermute(value[:, unit:].astype(BF16), ("occ", "vir"), pairs)
        return (value[:, :unit] + got.astype(F32)).astype(BF16)

    moved = swap(back(first, 1, 3), "occ", 2)
    kept = back(second, 3, 1)
    shape = (aux, occ_dev, vir)
    out_alpha = jnp.where(core == 1, moved, kept).reshape(shape)
    out_beta = jnp.where(core == 1, kept, moved).reshape(shape)
    return out_alpha, out_beta


def solution(mesh):
    in_specs = (
        P("occ", None, "vir"),
        P("occ", None, "vir"),
        P("vir", None),
        P("occ"),
        P(),
        P(),
        P("vir"),
    )
    out_specs = (P(None, "occ", "vir"), P(None, "occ", "vir"))
    return jax.shard_map(ring, mesh=mesh, in_specs=in_specs, out_specs=out_specs, check_vma=False)
```

```python
import jax
import jax.numpy as jnp
from jax import lax
from jax.experimental import pallas as pl
from jax.experimental.pallas import tpu as pltpu
from jax.sharding import PartitionSpec as P

BF16, F32 = jnp.bfloat16, jnp.float32
VMEM = pl.BlockSpec(memory_space=pltpu.VMEM)
SMEM = pl.BlockSpec(memory_space=pltpu.SMEM)


def swap(value, axis, mask):
    pairs = [(source, source ^ mask) for source in range(lax.axis_size(axis))]
    return lax.ppermute(value, axis, pairs)


def alpha_of(device):
    return device ^ (2 * (device & 1))


def beta_of(device):
    return device ^ (2 * (1 - (device & 1)))


def shape_of(*dims, dtype=BF16):
    return jax.ShapeDtypeStruct(dims, dtype)


def call(kernel, shapes, *args, scratch=(), flops=0, specs=None):
    return pl.pallas_call(
        kernel,
        out_shape=shapes,
        in_specs=specs or [VMEM] * len(args),
        out_specs=jax.tree.map(lambda _: VMEM, shapes),
        scratch_shapes=scratch,
        cost_estimate=pl.CostEstimate(
            flops=flops, bytes_accessed=1 << 20, transcendentals=0
        ),
        compiler_params=pltpu.CompilerParams(vmem_limit_bytes=20 << 20),
    )(*args)


def dots(a, b, da, db):
    return lax.dot_general(a, b, (((da,), (db,)), ((), ())), preferred_element_type=F32)


def at(start, size):
    return pl.ds(pl.multiple_of(start, size), size)


def split_rows(index_of, chips, source, *refs):
    outs, table = refs[:-1], refs[-1]
    rows, blocks, cols = source.shape
    step = 16
    wide = step * blocks
    to = lax.broadcasted_iota(jnp.int32, (wide, wide), 0)
    by = lax.broadcasted_iota(jnp.int32, (wide, wide), 1)
    pick = jnp.where(by == (to % step) * blocks + to // step, 1.0, 0.0).astype(BF16)
    for q in range(0, rows, step):
        tile = dots(pick, source[q : q + step].reshape(wide, cols), 1, 0).astype(BF16)
        for d in range(blocks):
            table[d, q : q + step, :] = tile[d * step : (d + 1) * step]
    chip = lax.axis_index("occ") // 2
    for m in range(chips):
        for c in (0, 1):
            outs[m][c] = table[index_of(2 * (chip ^ m) + c)]


def give_rows(*refs):
    held, out = refs[:-1], refs[-1]
    core = lax.axis_index("occ") % 2
    for m, ref in enumerate(held):
        out[m] = ref[1 - core]


def place_rows(chips, *refs):
    held, take, out = refs[:chips], refs[chips], refs[-1]
    rows = take.shape[1]
    me = lax.axis_index("occ")
    chip, core = me // 2, me % 2
    for m in range(chips):
        start = 2 * (chip ^ m) * rows
        out[at(start + core * rows, rows), :] = held[m][core]
        out[at(start + (1 - core) * rows, rows), :] = take[m]


def regroup(ints, index_of):
    blocks = lax.axis_size("occ")
    chips = blocks // 2
    rows, _, cols = ints.shape
    if chips > 4:
        table = ints.transpose(1, 0, 2)
        table = jnp.stack([table[index_of(d)] for d in range(blocks)])
        got = lax.all_to_all(table, "occ", split_axis=0, concat_axis=0, tiled=True)
        return got.reshape(blocks * rows, cols)
    held = [*call(
        lambda *refs: split_rows(index_of, chips, *refs),
        [shape_of(2, rows, cols)] * chips,
        ints,
        scratch=[pltpu.VMEM((blocks, rows, cols), BF16)],
    )]
    for m in range(1, chips):
        held[m] = swap(held[m], "occ", 2 * m)
    give = call(give_rows, shape_of(chips, rows, cols), *held)
    take = swap(give, "occ", 1)
    place = lambda *refs: place_rows(chips, *refs)
    return call(place, shape_of(blocks * rows, cols), *held, take)


def halves_metric(metric):
    rows = metric.shape[0]
    half = rows // 2
    core, layer = lax.axis_index("occ") % 2, lax.axis_index("vir")
    mine = lax.dynamic_slice_in_dim(metric, core * half, half, 0)
    got = jnp.stack([swap(mine, "vir", k) for k in (1, 2, 3)])
    other = swap(got, "occ", 1)
    lo, hi = jnp.where(core == 0, got, other), jnp.where(core == 0, other, got)
    rest = jnp.concatenate([lo, hi], axis=1)
    pieces = [metric, rest[0], rest[1], rest[2]]
    return jnp.concatenate([lax.select_n(layer ^ k, *pieces) for k in range(4)], axis=0)


def place_metric(chips, *refs):
    own, mine, other, out = refs[0], refs[1 : 1 + chips], refs[1 + chips : 1 + 2 * chips], refs[-1]
    rows = own.shape[0]
    part = mine[0].shape[1]
    me, layer = lax.axis_index("occ"), lax.axis_index("vir")
    chip, core = me // 2, me % 2
    out[at(layer * rows, rows), :] = own[...]
    for k in (1, 2, 3):
        for m in range(chips):
            for c, held in ((core, mine), (1 - core, other)):
                start = (layer ^ k) * rows + (2 * (chip ^ m) + c) * part
                out[at(start, part), :] = held[m][k - 1]


def whole_metric(metric):
    rows, aux = metric.shape
    blocks = lax.axis_size("occ")
    chips = blocks // 2
    if chips > 4 or rows % (16 * blocks):
        return halves_metric(metric)
    part = rows // blocks
    mine = lax.dynamic_slice_in_dim(metric, lax.axis_index("occ") * part, part, 0)
    got = [swap(mine, "vir", k) for k in (1, 2, 3)]

    def pack(*refs):
        for k in range(3):
            refs[-1][k] = refs[k][...]

    got = call(pack, shape_of(3, part, aux), *got)
    plane = [got] + [swap(got, "occ", 2 * m) for m in range(1, chips)]
    other = [swap(p, "occ", 1) for p in plane]
    place = lambda *refs: place_metric(chips, *refs)
    return call(place, shape_of(aux, aux), metric, *plane, *other)


def row_chunks(rows, body, step=256):
    def one(i, carry):
        body(at(i * step, step))
        return carry

    lax.fori_loop(0, rows // step, one, 0)


def fit_rows(square, raw, out):
    def body(rows):
        out[rows, :] = dots(square[rows, :], raw[...], 1, 0).astype(BF16)

    row_chunks(square.shape[0], body)


def fit(square, raw):
    aux, unit = raw.shape
    return call(fit_rows, shape_of(aux, unit), square, raw, flops=2 * aux * aux * unit)


def tile_rows(occ_a, occ_o, occ_b, vir_a, vir_b, a0, a1, o0, o1, beta, amp, gamma, flip):
    layer, me = lax.axis_index("vir"), lax.axis_index("occ")
    unit = beta.shape[1]
    alphas = (a0, a1, o0, o1)
    flip[...] = beta[...].T
    right = occ_b[beta_of(me)] - vir_b[...]
    right = jnp.broadcast_to(right, (128, unit)).T[:, :1]
    for u, alpha in enumerate(alphas):
        row = vir_a[pl.ds(layer ^ (u % 2), 1), :]
        left = (occ_a, occ_a, occ_o, occ_o)[u][0] - row
        pair = dots(flip[...], alpha[...], 1, 0)
        amp[u] = (pair / (left + right)).astype(BF16)

    def body(rows):
        total = dots(a0[rows, :], amp[0], 1, 1)
        for u in (1, 2, 3):
            total = total + dots(alphas[u][rows, :], amp[u], 1, 1)
        gamma[rows, :] = total.astype(gamma.dtype)

    row_chunks(beta.shape[0], body)


def tile(energies, alphas, beta, dtype):
    aux, unit = beta.shape
    return call(
        tile_rows,
        [shape_of(4, unit, unit), shape_of(aux, unit, dtype=dtype)],
        *energies,
        *alphas,
        beta,
        scratch=[pltpu.VMEM((unit, aux), BF16)],
        flops=16 * aux * unit * unit,
        specs=[SMEM] * 3 + [VMEM] * 7,
    )


def term_rows(first, own, near, amp_own, amp_near, out):
    def body(rows):
        for u in (0, 1):
            cols = slice(u * own.shape[1], (u + 1) * own.shape[1])
            total = dots(own[rows, :], amp_own[first + u], 1, 0)
            total = total + dots(near[rows, :], amp_near[first + u], 1, 0)
            out[rows, cols] = total.astype(out.dtype)

    row_chunks(own.shape[0], body)


def term(first, own, near, amp_own, amp_near, dtype):
    aux, unit = own.shape
    kernel = lambda *refs: term_rows(first, *refs)
    shape = shape_of(aux, 2 * unit, dtype=dtype)
    flops = 8 * aux * unit * unit
    return call(kernel, shape, own, near, amp_own, amp_near, flops=flops)


def mix_rows(gamma_alpha, from_core, own, near, send_a, send_b, keep_a, keep_b):
    unit = own.shape[1]
    odd = lax.axis_index("occ") % 2 == 1

    def body(rows):
        alpha = gamma_alpha[rows, :] + from_core[rows, :].astype(F32)
        here, there = alpha[:, :unit], alpha[:, unit:].astype(BF16)
        beta, far = own[rows, :], near[rows, :]
        keep_a[rows, :] = jnp.where(odd, here, beta)
        keep_b[rows, :] = jnp.where(odd, beta, here)
        send_a[rows, :] = jnp.where(odd, there, far)
        send_b[rows, :] = jnp.where(odd, far, there)

    row_chunks(own.shape[0], body)


def ring(ints_alpha, ints_beta, metric, e_occ_alpha, e_occ_beta, e_vir_alpha, e_vir_beta):
    aux = metric.shape[1]
    unit = e_vir_beta.shape[0]
    blocks, layers = lax.axis_size("occ"), lax.axis_size("vir")
    assert layers == 4 and e_occ_alpha.shape[0] == 1
    core = lax.axis_index("occ") % 2

    square = whole_metric(metric)
    raw_beta = regroup(ints_beta, beta_of)
    raw_alpha = regroup(ints_alpha, alpha_of)

    occ_mine = lax.ppermute(e_occ_alpha, "occ", [(alpha_of(d), d) for d in range(blocks)])
    occ_other = swap(occ_mine, "occ", 1)
    vir_near = swap(e_vir_beta, "vir", 3)
    common = [occ_mine, occ_other, e_occ_beta, e_vir_alpha.reshape(layers, unit)]

    near_beta = swap(raw_beta, "vir", 3)
    near_alpha = swap(raw_alpha, "vir", 1)

    a0 = fit(square, raw_alpha)
    b0 = fit(square, raw_beta)
    a1 = fit(square, near_alpha)
    o0, o1 = swap(a0, "occ", 1), swap(a1, "occ", 1)
    alphas = (a0, a1, o0, o1)
    amp_own, gamma_own = tile(common + [e_vir_beta[None]], alphas, b0, F32)
    b1 = fit(square, near_beta)
    amp_near, gamma_near = tile(common + [vir_near[None]], alphas, b1, BF16)
    other_term = term(2, b0, b1, amp_own, amp_near, BF16)
    from_core = swap(other_term, "occ", 1)
    mine_term = term(0, b0, b1, amp_own, amp_near, F32)
    send_a, send_b, keep_a, keep_b = call(
        mix_rows,
        [shape_of(aux, unit)] * 2 + [shape_of(aux, unit, dtype=F32)] * 2,
        mine_term,
        from_core,
        gamma_own,
        gamma_near,
    )

    def back(send, keep, odd, even):
        pairs = [
            (d * layers + v, d * layers + (v ^ (odd if d % 2 else even)))
            for d in range(blocks)
            for v in range(layers)
        ]
        got = lax.ppermute(send, ("occ", "vir"), pairs)
        return (keep + got.astype(F32)).astype(BF16)

    done_a = back(send_a, keep_a, 1, 3)
    moved = swap(done_a, "occ", 2)
    kept = back(send_b, keep_b, 3, 1)
    out_alpha = jnp.where(core == 1, moved, kept).reshape(aux, 1, unit)
    out_beta = jnp.where(core == 1, kept, moved).reshape(aux, 1, unit)
    return out_alpha, out_beta


def solution(mesh):
    in_specs = (
        P("occ", None, "vir"),
        P("occ", None, "vir"),
        P("vir", None),
        P("occ"),
        P(),
        P(),
        P("vir"),
    )
    out_specs = (P(None, "occ", "vir"), P(None, "occ", "vir"))

    return jax.shard_map(ring, mesh=mesh, in_specs=in_specs, out_specs=out_specs, check_vma=False)
```

```python
import jax
import jax.numpy as jnp
from jax import lax
from jax.experimental import pallas as pl
from jax.experimental.pallas import tpu as pltpu
from jax.sharding import PartitionSpec as P

BF16, F32 = jnp.bfloat16, jnp.float32
VMEM = pl.BlockSpec(memory_space=pltpu.VMEM)
SMEM = pl.BlockSpec(memory_space=pltpu.SMEM)


def swap(value, axis, mask):
    pairs = [(source, source ^ mask) for source in range(lax.axis_size(axis))]
    return lax.ppermute(value, axis, pairs)


def alpha_of(device):
    return device ^ (2 * (device & 1))


def beta_of(device):
    return device ^ (2 * (1 - (device & 1)))


def shape_of(*dims, dtype=BF16):
    return jax.ShapeDtypeStruct(dims, dtype)


def call(kernel, shapes, *args, scratch=(), flops=0, specs=None):
    return pl.pallas_call(
        kernel,
        out_shape=shapes,
        in_specs=specs or [VMEM] * len(args),
        out_specs=jax.tree.map(lambda _: VMEM, shapes),
        scratch_shapes=scratch,
        cost_estimate=pl.CostEstimate(
            flops=flops, bytes_accessed=1 << 20, transcendentals=0
        ),
        compiler_params=pltpu.CompilerParams(vmem_limit_bytes=16 << 20),
    )(*args)


def dots(a, b, da, db):
    return lax.dot_general(a, b, (((da,), (db,)), ((), ())), preferred_element_type=F32)


def at(start, size):
    return pl.ds(pl.multiple_of(start, size), size)


def split_rows(index_of, chips, source, *refs):
    outs, table = refs[:-1], refs[-1]
    rows, blocks, cols = source.shape
    step = 16
    wide = step * blocks
    to = lax.broadcasted_iota(jnp.int32, (wide, wide), 0)
    by = lax.broadcasted_iota(jnp.int32, (wide, wide), 1)
    pick = jnp.where(by == (to % step) * blocks + to // step, 1.0, 0.0).astype(BF16)
    for q in range(0, rows, step):
        tile = dots(pick, source[q : q + step].reshape(wide, cols), 1, 0).astype(BF16)
        for d in range(blocks):
            table[d, q : q + step, :] = tile[d * step : (d + 1) * step]
    chip = lax.axis_index("occ") // 2
    for m in range(chips):
        for c in (0, 1):
            outs[m][c] = table[index_of(2 * (chip ^ m) + c)]


def give_rows(*refs):
    held, out = refs[:-1], refs[-1]
    core = lax.axis_index("occ") % 2
    for m, ref in enumerate(held):
        out[m] = ref[1 - core]


def place_rows(chips, *refs):
    held, take, out = refs[:chips], refs[chips], refs[-1]
    rows = take.shape[1]
    me = lax.axis_index("occ")
    chip, core = me // 2, me % 2
    for m in range(chips):
        start = 2 * (chip ^ m) * rows
        out[at(start + core * rows, rows), :] = held[m][core]
        out[at(start + (1 - core) * rows, rows), :] = take[m]


def regroup(ints, index_of):
    blocks = lax.axis_size("occ")
    chips = blocks // 2
    rows, _, cols = ints.shape
    if chips > 4:
        table = ints.transpose(1, 0, 2)
        table = jnp.stack([table[index_of(d)] for d in range(blocks)])
        got = lax.all_to_all(table, "occ", split_axis=0, concat_axis=0, tiled=True)
        return got.reshape(blocks * rows, cols)
    held = [*call(
        lambda *refs: split_rows(index_of, chips, *refs),
        [shape_of(2, rows, cols)] * chips,
        ints,
        scratch=[pltpu.VMEM((blocks, rows, cols), BF16)],
    )]
    for m in range(1, chips):
        held[m] = swap(held[m], "occ", 2 * m)
    give = call(give_rows, shape_of(chips, rows, cols), *held)
    take = swap(give, "occ", 1)
    place = lambda *refs: place_rows(chips, *refs)
    return call(place, shape_of(blocks * rows, cols), *held, take)


def halves_metric(metric):
    rows = metric.shape[0]
    half = rows // 2
    core, layer = lax.axis_index("occ") % 2, lax.axis_index("vir")
    mine = lax.dynamic_slice_in_dim(metric, core * half, half, 0)
    got = jnp.stack([swap(mine, "vir", k) for k in (1, 2, 3)])
    other = swap(got, "occ", 1)
    lo, hi = jnp.where(core == 0, got, other), jnp.where(core == 0, other, got)
    rest = jnp.concatenate([lo, hi], axis=1)
    pieces = [metric, rest[0], rest[1], rest[2]]
    return jnp.concatenate([lax.select_n(layer ^ k, *pieces) for k in range(4)], axis=0)


def pack_metric(*refs):
    for k, ref in enumerate(refs[:-1]):
        refs[-1][k] = ref[...]


def cut_metric(by_x, by_y, via_x, via_y):
    half = via_x.shape[2]
    via_x[...] = by_y[:, :, :half]
    via_y[...] = by_x[:, :, half:]


def place_metric(own, *refs):
    refs, out = refs[:-1], refs[-1]
    mine, other = refs[: len(refs) // 2], refs[len(refs) // 2 :]
    rows = own.shape[0]
    part, half = mine[0].shape[1], mine[-1].shape[2]
    me, layer = lax.axis_index("occ"), lax.axis_index("vir")
    chip, core = me // 2, me % 2
    out[at(layer * rows, rows), :] = own[...]
    for k in (1, 2, 3):
        for c, held in ((core, mine), (1 - core, other)):
            start = lambda m: (layer ^ k) * rows + (2 * (chip ^ m) + c) * part
            for m in (0, 1, 2):
                out[at(start(m), part), :] = held[m][k - 1]
            out[at(start(3), part), :half] = held[3][k - 1]
            out[at(start(3), part), half:] = held[4][k - 1]


def whole_metric(metric):
    rows, aux = metric.shape
    blocks = lax.axis_size("occ")
    if blocks != 8 or rows % (16 * blocks) or aux % 256:
        return halves_metric(metric)
    part = rows // blocks
    mine = lax.dynamic_slice_in_dim(metric, lax.axis_index("occ") * part, part, 0)
    got = [swap(mine, "vir", k) for k in (1, 2, 3)]
    got = call(pack_metric, shape_of(3, part, aux), *got)
    by_x, by_y = swap(got, "occ", 2), swap(got, "occ", 4)
    halves = call(cut_metric, [shape_of(3, part, aux // 2)] * 2, by_x, by_y)
    via_x, via_y = swap(halves[0], "occ", 2), swap(halves[1], "occ", 4)
    plane = [got, by_x, by_y, via_x, via_y]
    other = [swap(p, "occ", 1) for p in plane]
    return call(place_metric, shape_of(aux, aux), metric, *plane, *other)


def row_chunks(rows, body, step=512):
    step = step if rows % step == 0 else rows
    for start in range(0, rows, step):
        body(slice(start, start + step))


def fit_rows(square, raw, out):
    def body(rows):
        out[rows, :] = dots(square[rows, :], raw[...], 1, 0).astype(BF16)

    row_chunks(square.shape[0], body)


def fit(square, raw):
    aux, unit = raw.shape
    return call(fit_rows, shape_of(aux, unit), square, raw, flops=2 * aux * aux * unit)


def tile_rows(occ_a, occ_o, occ_b, vir_a, vir_b, a0, a1, o0, o1, beta, amp, gamma, flip):
    layer, me = lax.axis_index("vir"), lax.axis_index("occ")
    unit = beta.shape[1]
    alphas = (a0, a1, o0, o1)
    flip[...] = beta[...].T
    right = occ_b[beta_of(me)] - vir_b[...]
    right = jnp.broadcast_to(right, (128, unit)).T[:, :1]
    for u, alpha in enumerate(alphas):
        row = vir_a[at((layer ^ (u % 2)) * unit, unit)].reshape(1, unit)
        left = (occ_a, occ_a, occ_o, occ_o)[u][0] - row
        pair = dots(flip[...], alpha[...], 1, 0)
        amp[u] = (pair / (left + right)).astype(BF16)

    def body(rows):
        total = dots(a0[rows, :], amp[0], 1, 1)
        for u in (1, 2, 3):
            total = total + dots(alphas[u][rows, :], amp[u], 1, 1)
        gamma[rows, :] = total.astype(gamma.dtype)

    row_chunks(beta.shape[0], body)


def tile(energies, alphas, beta, dtype):
    aux, unit = beta.shape
    return call(
        tile_rows,
        [shape_of(4, unit, unit), shape_of(aux, unit, dtype=dtype)],
        *energies,
        *alphas,
        beta,
        scratch=[pltpu.VMEM((unit, aux), BF16)],
        flops=16 * aux * unit * unit,
        specs=[SMEM] * 3 + [VMEM] * 7,
    )


def term_rows(first, own, near, amp_own, amp_near, out):
    def body(rows):
        for u in (0, 1):
            cols = slice(u * own.shape[1], (u + 1) * own.shape[1])
            total = dots(own[rows, :], amp_own[first + u], 1, 0)
            total = total + dots(near[rows, :], amp_near[first + u], 1, 0)
            out[rows, cols] = total.astype(out.dtype)

    row_chunks(own.shape[0], body)


def term(first, own, near, amp_own, amp_near, dtype):
    aux, unit = own.shape
    kernel = lambda *refs: term_rows(first, *refs)
    shape = shape_of(aux, 2 * unit, dtype=dtype)
    flops = 8 * aux * unit * unit
    return call(kernel, shape, own, near, amp_own, amp_near, flops=flops)


def mix_rows(gamma_alpha, from_core, own, near, send_a, send_b, keep_a, keep_b):
    unit = own.shape[1]
    odd = lax.axis_index("occ") % 2 == 1

    def body(rows):
        alpha = gamma_alpha[rows, :] + from_core[rows, :].astype(F32)
        here, there = alpha[:, :unit], alpha[:, unit:].astype(BF16)
        beta, far = own[rows, :], near[rows, :]
        keep_a[rows, :] = jnp.where(odd, here, beta)
        keep_b[rows, :] = jnp.where(odd, beta, here)
        send_a[rows, :] = jnp.where(odd, there, far)
        send_b[rows, :] = jnp.where(odd, far, there)

    row_chunks(own.shape[0], body)


def ring(ints_alpha, ints_beta, metric, e_occ_alpha, e_occ_beta, e_vir_alpha, e_vir_beta):
    aux = metric.shape[1]
    unit = e_vir_beta.shape[0]
    blocks, layers = lax.axis_size("occ"), lax.axis_size("vir")
    assert layers == 4 and e_occ_alpha.shape[0] == 1
    core = lax.axis_index("occ") % 2

    square = whole_metric(metric)
    raw_beta = regroup(ints_beta, beta_of)
    raw_alpha = regroup(ints_alpha, alpha_of)

    occ_mine = lax.ppermute(e_occ_alpha, "occ", [(alpha_of(d), d) for d in range(blocks)])
    vir_near = swap(e_vir_beta, "vir", 3)
    occ_other = swap(occ_mine, "occ", 1)
    common = [occ_mine, occ_other, e_occ_beta, e_vir_alpha]

    near_beta = swap(raw_beta, "vir", 3)
    near_alpha = swap(raw_alpha, "vir", 1)

    a0 = fit(square, raw_alpha)
    b0 = fit(square, raw_beta)
    a1 = fit(square, near_alpha)
    o0, o1 = swap(a0, "occ", 1), swap(a1, "occ", 1)
    alphas = (a0, a1, o0, o1)
    amp_own, gamma_own = tile(common + [e_vir_beta[None]], alphas, b0, F32)
    b1 = fit(square, near_beta)
    amp_near, gamma_near = tile(common + [vir_near[None]], alphas, b1, BF16)
    other_term = term(2, b0, b1, amp_own, amp_near, BF16)
    from_core = swap(other_term, "occ", 1)
    mine_term = term(0, b0, b1, amp_own, amp_near, F32)
    send_a, send_b, keep_a, keep_b = call(
        mix_rows,
        [shape_of(aux, unit)] * 2 + [shape_of(aux, unit, dtype=F32)] * 2,
        mine_term,
        from_core,
        gamma_own,
        gamma_near,
    )

    def back(send, keep, odd, even):
        pairs = [
            (d * layers + v, d * layers + (v ^ (odd if d % 2 else even)))
            for d in range(blocks)
            for v in range(layers)
        ]
        got = lax.ppermute(send, ("occ", "vir"), pairs)
        return (keep + got.astype(F32)).astype(BF16)

    done_a = back(send_a, keep_a, 1, 3)
    moved = swap(done_a, "occ", 2)
    kept = back(send_b, keep_b, 3, 1)
    out_alpha = jnp.where(core == 1, moved, kept).reshape(aux, 1, unit)
    out_beta = jnp.where(core == 1, kept, moved).reshape(aux, 1, unit)
    return out_alpha, out_beta


def solution(mesh):
    in_specs = (
        P("occ", None, "vir"),
        P("occ", None, "vir"),
        P("vir", None),
        P("occ"),
        P(),
        P(),
        P("vir"),
    )
    out_specs = (P(None, "occ", "vir"), P(None, "occ", "vir"))

    return jax.shard_map(ring, mesh=mesh, in_specs=in_specs, out_specs=out_specs, check_vma=False)
```

```python
import jax
import jax.numpy as jnp
from jax import lax
from jax.experimental import pallas as pl
from jax.experimental.pallas import tpu as pltpu
from jax.sharding import PartitionSpec as P

BF16, F32 = jnp.bfloat16, jnp.float32
VMEM = pl.BlockSpec(memory_space=pltpu.VMEM)
SMEM = pl.BlockSpec(memory_space=pltpu.SMEM)


def swap(value, axis, mask):
    pairs = [(source, source ^ mask) for source in range(lax.axis_size(axis))]
    return lax.ppermute(value, axis, pairs)


def alpha_of(device):
    return device ^ (2 * (device & 1))


def beta_of(device):
    return device ^ (2 * (1 - (device & 1)))


def shape_of(*dims, dtype=BF16):
    return jax.ShapeDtypeStruct(dims, dtype)


def call(kernel, shapes, *args, scratch=(), flops=0, specs=None):
    return pl.pallas_call(
        kernel,
        out_shape=shapes,
        in_specs=specs or [VMEM] * len(args),
        out_specs=jax.tree.map(lambda _: VMEM, shapes),
        scratch_shapes=scratch,
        cost_estimate=pl.CostEstimate(
            flops=flops, bytes_accessed=1 << 20, transcendentals=0
        ),
        compiler_params=pltpu.CompilerParams(vmem_limit_bytes=16 << 20),
    )(*args)


def dots(a, b, da, db):
    return lax.dot_general(a, b, (((da,), (db,)), ((), ())), preferred_element_type=F32)


def at(start, size):
    return pl.ds(pl.multiple_of(start, size), size)


def split_rows(index_of, chips, source, *refs):
    outs, table = refs[:-1], refs[-1]
    rows, blocks, cols = source.shape
    step = 16
    wide = step * blocks
    to = lax.broadcasted_iota(jnp.int32, (wide, wide), 0)
    by = lax.broadcasted_iota(jnp.int32, (wide, wide), 1)
    pick = jnp.where(by == (to % step) * blocks + to // step, 1.0, 0.0).astype(BF16)
    for q in range(0, rows, step):
        tile = dots(pick, source[q : q + step].reshape(wide, cols), 1, 0).astype(BF16)
        for d in range(blocks):
            table[d, q : q + step, :] = tile[d * step : (d + 1) * step]
    chip = lax.axis_index("occ") // 2
    for m in range(chips):
        for c in (0, 1):
            outs[m][c] = table[index_of(2 * (chip ^ m) + c)]


def give_rows(*refs):
    held, out = refs[:-1], refs[-1]
    core = lax.axis_index("occ") % 2
    for m, ref in enumerate(held):
        out[m] = ref[1 - core]


def place_rows(chips, *refs):
    held, take, outs = refs[:chips], refs[chips], refs[chips + 1 :]
    rows = take.shape[1]
    me = lax.axis_index("occ")
    chip, core = me // 2, me % 2
    for m in range(chips):
        start = 2 * (chip ^ m) * rows
        for i, out in enumerate(outs):
            cols = slice(i * out.shape[1], (i + 1) * out.shape[1])
            out[at(start + core * rows, rows), :] = held[m][core, :, cols]
            out[at(start + (1 - core) * rows, rows), :] = take[m, :, cols]


def regroup(ints, index_of, parts):
    blocks = lax.axis_size("occ")
    chips = blocks // 2
    rows, _, cols = ints.shape
    if chips > 4:
        table = ints.transpose(1, 0, 2)
        table = jnp.stack([table[index_of(d)] for d in range(blocks)])
        got = lax.all_to_all(table, "occ", split_axis=0, concat_axis=0, tiled=True)
        return jnp.split(got.reshape(blocks * rows, cols), parts, axis=1)
    held = [*call(
        lambda *refs: split_rows(index_of, chips, *refs),
        [shape_of(2, rows, cols)] * chips,
        ints,
        scratch=[pltpu.VMEM((blocks, rows, cols), BF16)],
    )]
    for m in range(1, chips):
        held[m] = swap(held[m], "occ", 2 * m)
    give = call(give_rows, shape_of(chips, rows, cols), *held)
    take = swap(give, "occ", 1)
    place = lambda *refs: place_rows(chips, *refs)
    shapes = [shape_of(blocks * rows, cols // parts)] * parts
    return call(place, shapes, *held, take)


def halves_metric(metric):
    rows = metric.shape[0]
    half = rows // 2
    core, layer = lax.axis_index("occ") % 2, lax.axis_index("vir")
    mine = lax.dynamic_slice_in_dim(metric, core * half, half, 0)
    got = jnp.stack([swap(mine, "vir", k) for k in (1, 2, 3)])
    other = swap(got, "occ", 1)
    lo, hi = jnp.where(core == 0, got, other), jnp.where(core == 0, other, got)
    rest = jnp.concatenate([lo, hi], axis=1)
    pieces = [metric, rest[0], rest[1], rest[2]]
    return jnp.concatenate([lax.select_n(layer ^ k, *pieces) for k in range(4)], axis=0)


def pack_metric(*refs):
    for k, ref in enumerate(refs[:-1]):
        refs[-1][k] = ref[...]


def cut_metric(by_x, by_y, via_x, via_y):
    half = via_x.shape[2]
    via_x[...] = by_y[:, :, :half]
    via_y[...] = by_x[:, :, half:]


def place_metric(own, *refs):
    refs, out = refs[:-1], refs[-1]
    mine, other = refs[: len(refs) // 2], refs[len(refs) // 2 :]
    rows = own.shape[0]
    part, half = mine[0].shape[1], mine[-1].shape[2]
    me, layer = lax.axis_index("occ"), lax.axis_index("vir")
    chip, core = me // 2, me % 2
    out[at(layer * rows, rows), :] = own[...]
    for k in (1, 2, 3):
        for c, held in ((core, mine), (1 - core, other)):
            start = lambda m: (layer ^ k) * rows + (2 * (chip ^ m) + c) * part
            for m in (0, 1, 2):
                out[at(start(m), part), :] = held[m][k - 1]
            out[at(start(3), part), :half] = held[3][k - 1]
            out[at(start(3), part), half:] = held[4][k - 1]


def whole_metric(metric):
    rows, aux = metric.shape
    blocks = lax.axis_size("occ")
    if blocks != 8 or rows % (16 * blocks) or aux % 256:
        return halves_metric(metric)
    part = rows // blocks
    mine = lax.dynamic_slice_in_dim(metric, lax.axis_index("occ") * part, part, 0)
    got = [swap(mine, "vir", k) for k in (1, 2, 3)]
    got = call(pack_metric, shape_of(3, part, aux), *got)
    by_x, by_y = swap(got, "occ", 2), swap(got, "occ", 4)
    halves = call(cut_metric, [shape_of(3, part, aux // 2)] * 2, by_x, by_y)
    via_x, via_y = swap(halves[0], "occ", 2), swap(halves[1], "occ", 4)
    plane = [got, by_x, by_y, via_x, via_y]
    other = [swap(p, "occ", 1) for p in plane]
    return call(place_metric, shape_of(aux, aux), metric, *plane, *other)


def row_chunks(rows, body, step=512):
    step = step if rows % step == 0 else rows
    for start in range(0, rows, step):
        body(slice(start, start + step))


def fit_rows(square, *refs):
    raws, out = refs[:-1], refs[-1]
    raw = jnp.concatenate([r[...] for r in raws], axis=1)

    def body(rows):
        out[rows, :] = dots(square[rows, :], raw, 1, 0).astype(BF16)

    row_chunks(square.shape[0], body)


def fit(square, *raws):
    aux = square.shape[0]
    unit = sum(raw.shape[1] for raw in raws)
    return call(fit_rows, shape_of(aux, unit), square, *raws, flops=2 * aux * aux * unit)


def energy_rows(occ_a, occ_o, occ_b, vir_a, vir_b, vir_n, left, right, *near):
    layer, me = lax.axis_index("vir"), lax.axis_index("occ")
    unit = vir_b.shape[1]
    for u, occ in enumerate((occ_a, occ_a, occ_o, occ_o)):
        row = vir_a[at((layer ^ (u % 2)) * unit, unit)].reshape(1, unit)
        left[u : u + 1, :] = occ[0] - row
    column = lambda vir: jnp.broadcast_to(occ_b[beta_of(me)] - vir[...], (128, unit)).T
    right[...] = column(vir_b)
    half = unit // 2
    for i, out in enumerate(near):
        out[...] = column(vir_n)[i * half : (i + 1) * half]


def tile_rows(a0, a1, o0, o1, beta, left, right, amp, gamma, flip):
    alphas = (a0, a1, o0, o1)
    flip[...] = beta[...].T
    column = right[:, :1]
    for u, alpha in enumerate(alphas):
        pair = dots(flip[...], alpha[...], 1, 0)
        amp[u] = (pair / (left[u : u + 1, :] + column)).astype(BF16)

    def body(rows):
        total = dots(a0[rows, :], amp[0], 1, 1)
        for u in (1, 2, 3):
            total = total + dots(alphas[u][rows, :], amp[u], 1, 1)
        gamma[rows, :] = total.astype(gamma.dtype)

    row_chunks(beta.shape[0], body)


def tile(alphas, beta, left, right, dtype):
    aux, width = beta.shape
    unit = alphas[0].shape[1]
    return call(
        tile_rows,
        [shape_of(4, width, unit), shape_of(aux, width, dtype=dtype)],
        *alphas,
        beta,
        left,
        right,
        scratch=[pltpu.VMEM((width, aux), BF16)],
        flops=16 * aux * unit * width,
    )


def early_rows(own, near, amp_own, amp_near, out):
    unit = amp_own.shape[2]

    def body(rows):
        for u in range(4):
            total = dots(own[rows, :], amp_own[u], 1, 0) + dots(near[rows, :], amp_near[u], 1, 0)
            out[rows, u * unit : (u + 1) * unit] = total

    row_chunks(own.shape[0], body)


def late_rows(early, near, amp, out):
    unit = amp.shape[2]

    def body(rows):
        for u in (0, 1):
            total = early[rows, (2 + u) * unit : (3 + u) * unit] + dots(near[rows, :], amp[2 + u], 1, 0)
            out[rows, u * unit : (u + 1) * unit] = total.astype(BF16)

    row_chunks(near.shape[0], body)


def mix_rows(early, near, amp, core_term, own_gamma, near_gamma, *outs):
    unit = amp.shape[2]
    half = unit // 2
    odd = lax.axis_index("occ") % 2 == 1

    def body(rows):
        alpha = []
        for u in (0, 1):
            cols = slice(u * unit, (u + 1) * unit)
            total = early[rows, cols] + dots(near[rows, :], amp[u], 1, 0)
            alpha.append(total + core_term[rows, cols].astype(F32))
        here, there = alpha[0], alpha[1].astype(BF16)
        beta, far = own_gamma[rows, half:], near_gamma[rows, :]
        pick = lambda a, b: jnp.where(odd, a, b)
        outs[0][rows, :] = pick(there[:, :half], far)
        outs[1][rows, :] = pick(there[:, half:], there[:, :half])
        outs[2][rows, :] = pick(far, there[:, half:])
        outs[3][rows, :] = pick(here[:, :half], beta)
        outs[4][rows, :] = pick(here[:, half:], here[:, :half])
        outs[5][rows, :] = pick(beta, here[:, half:])

    row_chunks(near.shape[0], body, 256)


def sum_one(own_gamma, got, out):
    out[...] = (own_gamma[:, : out.shape[1]] + got[...].astype(F32)).astype(BF16)


def sum_two(keep, got, first, out, send):
    odd = lax.axis_index("occ") % 2 == 1
    total = (keep[...] + got[...].astype(F32)).astype(BF16)
    out[...] = total
    send[...] = jnp.where(odd, total, first[...])


def sum_three(keep, got, second, out, send):
    odd = lax.axis_index("occ") % 2 == 1
    total = (keep[...] + got[...].astype(F32)).astype(BF16)
    out[...] = total
    send[...] = jnp.where(odd, total, second[...])


def last_rows(keep, got, first, third, move_a, move_b, alpha, beta):
    odd = lax.axis_index("occ") % 2 == 1
    half = keep.shape[1]
    final = (keep[...] + got[...].astype(F32)).astype(BF16)
    side = jnp.where(odd, first[...], third[...])
    a, b = move_a[...], move_b[...]
    alpha[:, :half] = jnp.where(odd, a, side)
    alpha[:, half:] = jnp.where(odd, b, final)
    beta[:, :half] = jnp.where(odd, side, a)
    beta[:, half:] = jnp.where(odd, final, b)


def last(*arrays):
    aux, half = arrays[0].shape
    step = 256 if aux % 256 == 0 else aux
    spec = lambda width: pl.BlockSpec((step, width), lambda i: (i, 0))
    return pl.pallas_call(
        last_rows,
        grid=(aux // step,),
        out_shape=[shape_of(aux, 2 * half)] * 2,
        in_specs=[spec(half)] * len(arrays),
        out_specs=[spec(2 * half)] * 2,
        compiler_params=pltpu.CompilerParams(vmem_limit_bytes=8 << 20),
    )(*arrays)


def ring(ints_alpha, ints_beta, metric, e_occ_alpha, e_occ_beta, e_vir_alpha, e_vir_beta):
    aux = metric.shape[1]
    unit = e_vir_beta.shape[0]
    half = unit // 2
    blocks, layers = lax.axis_size("occ"), lax.axis_size("vir")
    assert layers == 4 and e_occ_alpha.shape[0] == 1

    square = whole_metric(metric)
    raw_beta = regroup(ints_beta, beta_of, 2)
    (raw_alpha,) = regroup(ints_alpha, alpha_of, 1)

    occ_mine = lax.ppermute(e_occ_alpha, "occ", [(alpha_of(d), d) for d in range(blocks)])
    vir_near = swap(e_vir_beta, "vir", 3)
    occ_other = swap(occ_mine, "occ", 1)
    left, right, right_zero, right_one = call(
        energy_rows,
        [shape_of(4, unit, dtype=F32)] + [shape_of(n, 128, dtype=F32) for n in (unit, half, half)],
        occ_mine,
        occ_other,
        e_occ_beta,
        e_vir_alpha,
        e_vir_beta[None],
        vir_near[None],
        specs=[SMEM] * 3 + [VMEM] * 3,
    )

    near_beta = []
    for raw in raw_beta:
        near_beta.append(swap(raw, "vir", 3))
    near_alpha = swap(raw_alpha, "vir", 1)

    a0 = fit(square, raw_alpha)
    o0 = swap(a0, "occ", 1)
    b0 = fit(square, *raw_beta)
    a1 = fit(square, near_alpha)
    o1 = swap(a1, "occ", 1)
    alphas = (a0, a1, o0, o1)
    amp_own, gamma_own = tile(alphas, b0, left, right, F32)
    b1 = fit(square, near_beta[0])
    amp_zero, gamma_zero = tile(alphas, b1, left, right_zero, BF16)

    def back(send, odd, even):
        pairs = [
            (d * layers + v, d * layers + (v ^ (odd if d % 2 else even)))
            for d in range(blocks)
            for v in range(layers)
        ]
        return lax.ppermute(send, ("occ", "vir"), pairs)

    got_one = back(gamma_zero, 3, 3)
    wide = shape_of(aux, 4 * unit, dtype=F32)
    early = call(early_rows, wide, b0, b1, amp_own, amp_zero, flops=12 * aux * unit * unit)
    b2 = fit(square, near_beta[1])
    amp_one, gamma_one = tile(alphas, b2, left, right_one, BF16)
    pair = shape_of(aux, 2 * unit)
    term = call(late_rows, pair, early, b2, amp_one, flops=2 * aux * unit * unit)
    from_core = swap(term, "occ", 1)
    thin, thin32 = shape_of(aux, half), shape_of(aux, half, dtype=F32)
    send2, send3, send4, keep2, keep3, keep4 = call(
        mix_rows,
        [thin] * 3 + [thin32] * 3,
        early,
        b2,
        amp_one,
        from_core,
        gamma_own,
        gamma_one,
        flops=2 * aux * unit * unit,
    )
    got_two = back(send2, 1, 3)
    got_three = back(send3, 1, 1)
    got_four = back(send4, 3, 1)
    first = call(sum_one, thin, gamma_own, got_one)
    second, send_a = call(sum_two, [thin] * 2, keep2, got_two, first)
    move_a = swap(send_a, "occ", 2)
    third, send_b = call(sum_three, [thin] * 2, keep3, got_three, second)
    move_b = swap(send_b, "occ", 2)
    out_alpha, out_beta = last(keep4, got_four, first, third, move_a, move_b)
    return out_alpha.reshape(aux, 1, unit), out_beta.reshape(aux, 1, unit)


def solution(mesh):
    in_specs = (
        P("occ", None, "vir"),
        P("occ", None, "vir"),
        P("vir", None),
        P("occ"),
        P(),
        P(),
        P("vir"),
    )
    out_specs = (P(None, "occ", "vir"), P(None, "occ", "vir"))

    return jax.shard_map(ring, mesh=mesh, in_specs=in_specs, out_specs=out_specs, check_vma=False)
```

```python
import jax
import jax.numpy as jnp
from jax import lax
from jax.experimental import pallas as pl
from jax.experimental.pallas import tpu as pltpu
from jax.sharding import PartitionSpec as P

BF16, F32 = jnp.bfloat16, jnp.float32
VMEM = pl.BlockSpec(memory_space=pltpu.VMEM)
SMEM = pl.BlockSpec(memory_space=pltpu.SMEM)


def swap(value, axis, mask):
    pairs = [(source, source ^ mask) for source in range(lax.axis_size(axis))]
    return lax.ppermute(value, axis, pairs)


def alpha_of(device):
    return device ^ (2 * (device & 1))


def beta_of(device):
    return device ^ (2 * (1 - (device & 1)))


def shape_of(*dims, dtype=BF16):
    return jax.ShapeDtypeStruct(dims, dtype)


def call(kernel, shapes, *args, scratch=(), flops=0, specs=None):
    return pl.pallas_call(
        kernel,
        out_shape=shapes,
        in_specs=specs or [VMEM] * len(args),
        out_specs=jax.tree.map(lambda _: VMEM, shapes),
        scratch_shapes=scratch,
        cost_estimate=pl.CostEstimate(
            flops=flops, bytes_accessed=1 << 20, transcendentals=0
        ),
        compiler_params=pltpu.CompilerParams(vmem_limit_bytes=16 << 20),
    )(*args)


def dots(a, b, da, db):
    return lax.dot_general(a, b, (((da,), (db,)), ((), ())), preferred_element_type=F32)


def at(start, size):
    return pl.ds(pl.multiple_of(start, size), size)


def split_rows(index_of, chips, source, *refs):
    outs, table = refs[:-1], refs[-1]
    rows, blocks, cols = source.shape
    step = 16
    wide = step * blocks
    to = lax.broadcasted_iota(jnp.int32, (wide, wide), 0)
    by = lax.broadcasted_iota(jnp.int32, (wide, wide), 1)
    pick = jnp.where(by == (to % step) * blocks + to // step, 1.0, 0.0).astype(BF16)
    for q in range(0, rows, step):
        tile = dots(pick, source[q : q + step].reshape(wide, cols), 1, 0).astype(BF16)
        for d in range(blocks):
            table[d, q : q + step, :] = tile[d * step : (d + 1) * step]
    chip = lax.axis_index("occ") // 2
    for m in range(chips):
        for c in (0, 1):
            outs[m][c] = table[index_of(2 * (chip ^ m) + c)]


def give_rows(*refs):
    held, out = refs[:-1], refs[-1]
    core = lax.axis_index("occ") % 2
    for m, ref in enumerate(held):
        out[m] = ref[1 - core]


def place_rows(chips, *refs):
    held, take, outs = refs[:chips], refs[chips], refs[chips + 1 :]
    rows = take.shape[1]
    me = lax.axis_index("occ")
    chip, core = me // 2, me % 2
    for m in range(chips):
        start = 2 * (chip ^ m) * rows
        for i, out in enumerate(outs):
            cols = slice(i * out.shape[1], (i + 1) * out.shape[1])
            out[at(start + core * rows, rows), :] = held[m][core, :, cols]
            out[at(start + (1 - core) * rows, rows), :] = take[m, :, cols]


def regroup(ints, index_of, parts):
    blocks = lax.axis_size("occ")
    chips = blocks // 2
    rows, _, cols = ints.shape
    if chips > 4:
        table = ints.transpose(1, 0, 2)
        table = jnp.stack([table[index_of(d)] for d in range(blocks)])
        got = lax.all_to_all(table, "occ", split_axis=0, concat_axis=0, tiled=True)
        return jnp.split(got.reshape(blocks * rows, cols), parts, axis=1)
    held = [*call(
        lambda *refs: split_rows(index_of, chips, *refs),
        [shape_of(2, rows, cols)] * chips,
        ints,
        scratch=[pltpu.VMEM((blocks, rows, cols), BF16)],
    )]
    for m in range(1, chips):
        held[m] = swap(held[m], "occ", 2 * m)
    give = call(give_rows, shape_of(chips, rows, cols), *held)
    take = swap(give, "occ", 1)
    place = lambda *refs: place_rows(chips, *refs)
    shapes = [shape_of(blocks * rows, cols // parts)] * parts
    return call(place, shapes, *held, take)


def halves_metric(metric):
    rows = metric.shape[0]
    half = rows // 2
    core, layer = lax.axis_index("occ") % 2, lax.axis_index("vir")
    mine = lax.dynamic_slice_in_dim(metric, core * half, half, 0)
    got = jnp.stack([swap(mine, "vir", k) for k in (1, 2, 3)])
    other = swap(got, "occ", 1)
    lo, hi = jnp.where(core == 0, got, other), jnp.where(core == 0, other, got)
    rest = jnp.concatenate([lo, hi], axis=1)
    pieces = [metric, rest[0], rest[1], rest[2]]
    return jnp.concatenate([lax.select_n(layer ^ k, *pieces) for k in range(4)], axis=0)


def pack_metric(*refs):
    for k, ref in enumerate(refs[:-1]):
        refs[-1][k] = ref[...]


def cut_metric(by_x, by_y, via_x, via_y):
    half = via_x.shape[2]
    via_x[...] = by_y[:, :, :half]
    via_y[...] = by_x[:, :, half:]


def place_metric(own, *refs):
    refs, out = refs[:-1], refs[-1]
    mine, other = refs[: len(refs) // 2], refs[len(refs) // 2 :]
    rows = own.shape[0]
    part, half = mine[0].shape[1], mine[-1].shape[2]
    me, layer = lax.axis_index("occ"), lax.axis_index("vir")
    chip, core = me // 2, me % 2
    out[at(layer * rows, rows), :] = own[...]
    for k in (1, 2, 3):
        for c, held in ((core, mine), (1 - core, other)):
            start = lambda m: (layer ^ k) * rows + (2 * (chip ^ m) + c) * part
            for m in (0, 1, 2):
                out[at(start(m), part), :] = held[m][k - 1]
            out[at(start(3), part), :half] = held[3][k - 1]
            out[at(start(3), part), half:] = held[4][k - 1]


def whole_metric(metric):
    rows, aux = metric.shape
    blocks = lax.axis_size("occ")
    if blocks != 8 or rows % (16 * blocks) or aux % 256:
        return halves_metric(metric)
    part = rows // blocks
    mine = lax.dynamic_slice_in_dim(metric, lax.axis_index("occ") * part, part, 0)
    got = [swap(mine, "vir", k) for k in (1, 2, 3)]
    got = call(pack_metric, shape_of(3, part, aux), *got)
    by_x, by_y = swap(got, "occ", 2), swap(got, "occ", 4)
    halves = call(cut_metric, [shape_of(3, part, aux // 2)] * 2, by_x, by_y)
    via_x, via_y = swap(halves[0], "occ", 2), swap(halves[1], "occ", 4)
    plane = [got, by_x, by_y, via_x, via_y]
    other = [swap(p, "occ", 1) for p in plane]
    return call(place_metric, shape_of(aux, aux), metric, *plane, *other)


def row_chunks(rows, body, step=512):
    step = step if rows % step == 0 else rows
    for start in range(0, rows, step):
        body(slice(start, start + step))


def fit_rows(square, *refs):
    raws, out = refs[:-1], refs[-1]
    raw = jnp.concatenate([r[...] for r in raws], axis=1)

    def body(rows):
        out[rows, :] = dots(square[rows, :], raw, 1, 0).astype(BF16)

    row_chunks(square.shape[0], body)


def fit(square, *raws):
    aux = square.shape[0]
    unit = sum(raw.shape[1] for raw in raws)
    return call(fit_rows, shape_of(aux, unit), square, *raws, flops=2 * aux * aux * unit)


def energy_rows(occ_a, occ_o, occ_b, vir_a, vir_b, vir_n, left, right, *near):
    layer, me = lax.axis_index("vir"), lax.axis_index("occ")
    unit = vir_b.shape[1]
    for u, occ in enumerate((occ_a, occ_a, occ_o, occ_o)):
        row = vir_a[at((layer ^ (u % 2)) * unit, unit)].reshape(1, unit)
        left[u : u + 1, :] = occ[0] - row
    column = lambda vir: jnp.broadcast_to(occ_b[beta_of(me)] - vir[...], (128, unit)).T
    right[...] = column(vir_b)
    half = unit // 2
    for i, out in enumerate(near):
        out[...] = column(vir_n)[i * half : (i + 1) * half]


def tile_rows(a0, a1, o0, o1, beta, left, right, amp, gamma, flip):
    alphas = (a0, a1, o0, o1)
    flip[...] = beta[...].T
    column = right[:, :1]
    for u, alpha in enumerate(alphas):
        pair = dots(flip[...], alpha[...], 1, 0)
        amp[u] = (pair / (left[u : u + 1, :] + column)).astype(BF16)

    def body(rows):
        total = dots(a0[rows, :], amp[0], 1, 1)
        for u in (1, 2, 3):
            total = total + dots(alphas[u][rows, :], amp[u], 1, 1)
        gamma[rows, :] = total.astype(gamma.dtype)

    row_chunks(beta.shape[0], body)


def tile(alphas, beta, left, right, dtype):
    aux, width = beta.shape
    unit = alphas[0].shape[1]
    return call(
        tile_rows,
        [shape_of(4, width, unit), shape_of(aux, width, dtype=dtype)],
        *alphas,
        beta,
        left,
        right,
        scratch=[pltpu.VMEM((width, aux), BF16)],
        flops=16 * aux * unit * width,
    )


def early_rows(own, near, amp_own, amp_near, out):
    unit = amp_own.shape[2]

    def body(rows):
        for u in range(4):
            total = dots(own[rows, :], amp_own[u], 1, 0) + dots(near[rows, :], amp_near[u], 1, 0)
            out[rows, u * unit : (u + 1) * unit] = total

    row_chunks(own.shape[0], body)


def late_rows(early, near, amp, out):
    unit = amp.shape[2]

    def body(rows):
        for u in (0, 1):
            total = early[rows, (2 + u) * unit : (3 + u) * unit] + dots(near[rows, :], amp[2 + u], 1, 0)
            out[rows, u * unit : (u + 1) * unit] = total.astype(BF16)

    row_chunks(near.shape[0], body)


def mix_rows(early, near, amp, core_term, own_gamma, near_gamma, *outs):
    unit = amp.shape[2]
    half = unit // 2
    odd = lax.axis_index("occ") % 2 == 1

    def body(rows):
        alpha = []
        for u in (0, 1):
            cols = slice(u * unit, (u + 1) * unit)
            total = early[rows, cols] + dots(near[rows, :], amp[u], 1, 0)
            alpha.append(total + core_term[rows, cols].astype(F32))
        here, there = alpha[0], alpha[1].astype(BF16)
        beta, far = own_gamma[rows, half:], near_gamma[rows, :]
        pick = lambda a, b: jnp.where(odd, a, b)
        outs[0][rows, :] = pick(there[:, :half], far)
        outs[1][rows, :] = pick(there[:, half:], there[:, :half])
        outs[2][rows, :] = pick(far, there[:, half:])
        outs[3][rows, :] = pick(here[:, :half], beta)
        outs[4][rows, :] = pick(here[:, half:], here[:, :half])
        outs[5][rows, :] = pick(beta, here[:, half:])

    row_chunks(near.shape[0], body, 256)


def sum_one(own_gamma, got, out):
    out[...] = (own_gamma[:, : out.shape[1]] + got[...].astype(F32)).astype(BF16)


def sum_two(keep, got, first, out, send):
    odd = lax.axis_index("occ") % 2 == 1
    total = (keep[...] + got[...].astype(F32)).astype(BF16)
    out[...] = total
    send[...] = jnp.where(odd, total, first[...])


def sum_three(keep, got, second, out, send):
    odd = lax.axis_index("occ") % 2 == 1
    total = (keep[...] + got[...].astype(F32)).astype(BF16)
    out[...] = total
    send[...] = jnp.where(odd, total, second[...])


def last_rows(keep, got, first, third, move_a, move_b, alpha, beta, hold_a, hold_b, sems):
    odd = lax.axis_index("occ") % 2 == 1
    aux, half = keep.shape
    step = aux // sems.shape[1]
    copies = []
    for i, start in enumerate(range(0, aux, step)):
        rows = slice(start, start + step)
        final = (keep[rows, :] + got[rows, :].astype(F32)).astype(BF16)
        side = jnp.where(odd, first[rows, :], third[rows, :])
        a, b = move_a[rows, :], move_b[rows, :]
        hold_a[rows, :half] = jnp.where(odd, a, side)
        hold_a[rows, half:] = jnp.where(odd, b, final)
        hold_b[rows, :half] = jnp.where(odd, side, a)
        hold_b[rows, half:] = jnp.where(odd, final, b)
        for j, (hold, out) in enumerate(((hold_a, alpha), (hold_b, beta))):
            copy = pltpu.make_async_copy(hold.at[rows, :], out.at[rows, :], sems.at[j, i])
            copy.start()
            copies.append(copy)
    for copy in copies:
        copy.wait()


def last(*arrays):
    aux, half = arrays[0].shape
    parts = 3
    anywhere = pl.BlockSpec(memory_space=pl.ANY)
    return pl.pallas_call(
        last_rows,
        out_shape=[shape_of(aux, 2 * half)] * 2,
        in_specs=[VMEM] * len(arrays),
        out_specs=[anywhere] * 2,
        scratch_shapes=[pltpu.VMEM((aux, 2 * half), BF16)] * 2
        + [pltpu.SemaphoreType.DMA((2, parts))],
        compiler_params=pltpu.CompilerParams(vmem_limit_bytes=8 << 20),
    )(*arrays)


def ring(ints_alpha, ints_beta, metric, e_occ_alpha, e_occ_beta, e_vir_alpha, e_vir_beta):
    aux = metric.shape[1]
    unit = e_vir_beta.shape[0]
    half = unit // 2
    blocks, layers = lax.axis_size("occ"), lax.axis_size("vir")
    assert layers == 4 and e_occ_alpha.shape[0] == 1

    square = whole_metric(metric)
    raw_beta = regroup(ints_beta, beta_of, 2)
    (raw_alpha,) = regroup(ints_alpha, alpha_of, 1)

    occ_mine = lax.ppermute(e_occ_alpha, "occ", [(alpha_of(d), d) for d in range(blocks)])
    vir_near = swap(e_vir_beta, "vir", 3)
    occ_other = swap(occ_mine, "occ", 1)
    left, right, right_zero, right_one = call(
        energy_rows,
        [shape_of(4, unit, dtype=F32)] + [shape_of(n, 128, dtype=F32) for n in (unit, half, half)],
        occ_mine,
        occ_other,
        e_occ_beta,
        e_vir_alpha,
        e_vir_beta[None],
        vir_near[None],
        specs=[SMEM] * 3 + [VMEM] * 3,
    )

    near_beta = []
    for raw in raw_beta:
        near_beta.append(swap(raw, "vir", 3))
    near_alpha = swap(raw_alpha, "vir", 1)

    a0 = fit(square, raw_alpha)
    o0 = swap(a0, "occ", 1)
    b0 = fit(square, *raw_beta)
    a1 = fit(square, near_alpha)
    o1 = swap(a1, "occ", 1)
    alphas = (a0, a1, o0, o1)
    amp_own, gamma_own = tile(alphas, b0, left, right, F32)
    b1 = fit(square, near_beta[0])
    amp_zero, gamma_zero = tile(alphas, b1, left, right_zero, BF16)

    def back(send, odd, even):
        pairs = [
            (d * layers + v, d * layers + (v ^ (odd if d % 2 else even)))
            for d in range(blocks)
            for v in range(layers)
        ]
        return lax.ppermute(send, ("occ", "vir"), pairs)

    got_one = back(gamma_zero, 3, 3)
    wide = shape_of(aux, 4 * unit, dtype=F32)
    early = call(early_rows, wide, b0, b1, amp_own, amp_zero, flops=12 * aux * unit * unit)
    b2 = fit(square, near_beta[1])
    amp_one, gamma_one = tile(alphas, b2, left, right_one, BF16)
    pair = shape_of(aux, 2 * unit)
    term = call(late_rows, pair, early, b2, amp_one, flops=2 * aux * unit * unit)
    from_core = swap(term, "occ", 1)
    thin, thin32 = shape_of(aux, half), shape_of(aux, half, dtype=F32)
    send2, send3, send4, keep2, keep3, keep4 = call(
        mix_rows,
        [thin] * 3 + [thin32] * 3,
        early,
        b2,
        amp_one,
        from_core,
        gamma_own,
        gamma_one,
        flops=2 * aux * unit * unit,
    )
    got_two = back(send2, 1, 3)
    got_three = back(send3, 1, 1)
    got_four = back(send4, 3, 1)
    first = call(sum_one, thin, gamma_own, got_one)
    second, send_a = call(sum_two, [thin] * 2, keep2, got_two, first)
    move_a = swap(send_a, "occ", 2)
    third, send_b = call(sum_three, [thin] * 2, keep3, got_three, second)
    move_b = swap(send_b, "occ", 2)
    out_alpha, out_beta = last(keep4, got_four, first, third, move_a, move_b)
    return out_alpha.reshape(aux, 1, unit), out_beta.reshape(aux, 1, unit)


def solution(mesh):
    in_specs = (
        P("occ", None, "vir"),
        P("occ", None, "vir"),
        P("vir", None),
        P("occ"),
        P(),
        P(),
        P("vir"),
    )
    out_specs = (P(None, "occ", "vir"), P(None, "occ", "vir"))

    return jax.shard_map(ring, mesh=mesh, in_specs=in_specs, out_specs=out_specs, check_vma=False)
```

```python
import jax
import jax.numpy as jnp
from jax import lax
from jax.experimental import pallas as pl
from jax.experimental.pallas import tpu as pltpu
from jax.sharding import PartitionSpec as P

BF16, F32 = jnp.bfloat16, jnp.float32
TAIL = 16
VMEM = pl.BlockSpec(memory_space=pltpu.VMEM)
SMEM = pl.BlockSpec(memory_space=pltpu.SMEM)


def swap(value, axis, mask):
    pairs = [(source, source ^ mask) for source in range(lax.axis_size(axis))]
    return lax.ppermute(value, axis, pairs)


def alpha_of(device):
    return device ^ (2 * (device & 1))


def beta_of(device):
    return device ^ (2 * (1 - (device & 1)))


def shape_of(*dims, dtype=BF16):
    return jax.ShapeDtypeStruct(dims, dtype)


def call(kernel, shapes, *args, scratch=(), flops=0, specs=None):
    return pl.pallas_call(
        kernel,
        out_shape=shapes,
        in_specs=specs or [VMEM] * len(args),
        out_specs=jax.tree.map(lambda _: VMEM, shapes),
        scratch_shapes=scratch,
        cost_estimate=pl.CostEstimate(
            flops=flops, bytes_accessed=1 << 20, transcendentals=0
        ),
        compiler_params=pltpu.CompilerParams(vmem_limit_bytes=16 << 20),
    )(*args)


def dots(a, b, da, db):
    return lax.dot_general(a, b, (((da,), (db,)), ((), ())), preferred_element_type=F32)


def at(start, size):
    return pl.ds(pl.multiple_of(start, size), size)


def split_rows(index_of, chips, source, *refs):
    outs, table = refs[:-1], refs[-1]
    rows, blocks, cols = source.shape
    step = 16
    wide = step * blocks
    to = lax.broadcasted_iota(jnp.int32, (wide, wide), 0)
    by = lax.broadcasted_iota(jnp.int32, (wide, wide), 1)
    pick = jnp.where(by == (to % step) * blocks + to // step, 1.0, 0.0).astype(BF16)
    for q in range(0, rows, step):
        tile = dots(pick, source[q : q + step].reshape(wide, cols), 1, 0).astype(BF16)
        for d in range(blocks):
            table[d, q : q + step, :] = tile[d * step : (d + 1) * step]
    chip = lax.axis_index("occ") // 2
    for m in range(chips):
        for c in (0, 1):
            outs[m][c] = table[index_of(2 * (chip ^ m) + c)]


def give_rows(*refs):
    held, out = refs[:-1], refs[-1]
    core = lax.axis_index("occ") % 2
    for m, ref in enumerate(held):
        out[m] = ref[1 - core]


def energy_tail(value, width):
    parts = []
    for _ in range(3):
        parts.append(value.astype(BF16).astype(F32))
        value = value - parts[-1]
    lines = [p[:, k : k + width] for p in parts for k in range(0, value.shape[1], width)]
    row = lax.broadcasted_iota(jnp.int32, (TAIL, width), 0)
    tail = jnp.zeros((TAIL, width), F32)
    for i, line in enumerate(lines):
        tail = jnp.where(row == i, jnp.broadcast_to(line, (TAIL, width)), tail)
    return tail.astype(BF16)


def energy_of(tail, unit):
    value = tail.astype(F32)
    step = unit // tail.shape[1]
    line = lambda i: value[i : i + 1] + value[i + step : i + step + 1] + value[i + 2 * step : i + 2 * step + 1]
    return jnp.concatenate([line(i) for i in range(step)], axis=1)


def tail_rows(energy, out):
    out[...] = energy_tail(energy[...], out.shape[1])


def place_rows(chips, extra, *refs):
    held, take, outs = refs[:chips], refs[chips], refs[chips + 1 + extra :]
    rows = take.shape[1]
    me = lax.axis_index("occ")
    chip, core = me // 2, me % 2
    for m in range(chips):
        start = 2 * (chip ^ m) * rows
        for i, out in enumerate(outs):
            cols = slice(i * out.shape[1], (i + 1) * out.shape[1])
            out[at(start + core * rows, rows), :] = held[m][core, :, cols]
            out[at(start + (1 - core) * rows, rows), :] = take[m, :, cols]
    if extra:
        out = outs[0]
        out[2 * chips * rows :, :] = energy_tail(refs[chips + 1][...], out.shape[1])


def regroup(ints, index_of, parts, *extra):
    blocks = lax.axis_size("occ")
    chips = blocks // 2
    rows, _, cols = ints.shape
    if chips > 4:
        table = ints.transpose(1, 0, 2)
        table = jnp.stack([table[index_of(d)] for d in range(blocks)])
        got = lax.all_to_all(table, "occ", split_axis=0, concat_axis=0, tiled=True)
        got = jnp.split(got.reshape(blocks * rows, cols), parts, axis=1)
        for energy in extra:
            tail = call(tail_rows, shape_of(TAIL, cols // parts), energy)
            got[0] = jnp.concatenate([got[0], tail], axis=0)
        return got
    held = [*call(
        lambda *refs: split_rows(index_of, chips, *refs),
        [shape_of(2, rows, cols)] * chips,
        ints,
        scratch=[pltpu.VMEM((blocks, rows, cols), BF16)],
    )]
    for m in range(1, chips):
        held[m] = swap(held[m], "occ", 2 * m)
    give = call(give_rows, shape_of(chips, rows, cols), *held)
    take = swap(give, "occ", 1)
    place = lambda *refs: place_rows(chips, len(extra), *refs)
    tails = [TAIL * len(extra)] + [0] * (parts - 1)
    shapes = [shape_of(blocks * rows + tail, cols // parts) for tail in tails]
    return call(place, shapes, *held, take, *extra)


def halves_metric(metric):
    rows = metric.shape[0]
    half = rows // 2
    core, layer = lax.axis_index("occ") % 2, lax.axis_index("vir")
    mine = lax.dynamic_slice_in_dim(metric, core * half, half, 0)
    got = jnp.stack([swap(mine, "vir", k) for k in (1, 2, 3)])
    other = swap(got, "occ", 1)
    lo, hi = jnp.where(core == 0, got, other), jnp.where(core == 0, other, got)
    rest = jnp.concatenate([lo, hi], axis=1)
    pieces = [metric, rest[0], rest[1], rest[2]]
    return jnp.concatenate([lax.select_n(layer ^ k, *pieces) for k in range(4)], axis=0)


def near_of(k):
    return k - 1 if k > 1 else 3


def cut_own(metric, *refs):
    outs, sems = refs[:-1], refs[-1]
    part, wide = outs[0].shape[0], outs[0].shape[1] // 2
    layer = lax.axis_index("vir")
    rows = at(lax.axis_index("occ") * part, part)
    copies = []
    for k, out in zip((1, 2, 3), outs):
        for i, block in enumerate((layer, layer ^ k ^ near_of(k))):
            source = metric.at[rows, at(block * wide, wide)]
            target = out.at[:, i * wide : (i + 1) * wide]
            copies.append(pltpu.make_async_copy(source, target, sems.at[k - 1, i]))
            copies[-1].start()
    for copy in copies:
        copy.wait()


def pack_metric(*refs):
    for k, ref in enumerate(refs[:-1]):
        refs[-1][k] = ref[...]


def cut_metric(by_x, by_y, via_x, via_y):
    half = via_x.shape[2]
    via_x[...] = by_y[:, :, :half]
    via_y[...] = by_x[:, :, half:]


def place_metric(own, *refs):
    refs, out, same, cross = refs[:-3], *refs[-3:]
    mine, other = refs[: len(refs) // 2], refs[len(refs) // 2 :]
    rows = own.shape[0]
    part = mine[0].shape[1]
    me, layer = lax.axis_index("occ"), lax.axis_index("vir")
    chip, core = me // 2, me % 2
    for k in (0, 1, 2):
        for c, held in ((core, mine), (1 - core, other)):
            for m in range(4):
                here = at((2 * (chip ^ m) + c) * part, part)
                same[k, here, :] = held[m][k, :, :rows]
                cross[k, here, :] = held[4 if m == 3 else m][k, :, -rows:]
    block = lambda u: at(u * rows, rows)
    out[block(layer), :] = own[...]
    for k in (1, 2, 3):
        there, third = layer ^ k, layer ^ near_of(k)
        out[block(there), block(there)] = same[k - 1]
        out[block(there), block(third)] = cross[k - 1]
        out[block(third), block(there)] = cross[k - 1].T
        out[block(there), block(layer)] = own[:, block(there)].T


def whole_metric(metric):
    rows, aux = metric.shape
    blocks = lax.axis_size("occ")
    if blocks != 8 or rows % (16 * blocks) or rows % 128 or aux != 4 * rows:
        return halves_metric(metric)
    part = rows // blocks
    mine = call(
        cut_own,
        [shape_of(part, 2 * rows)] * 3,
        metric,
        specs=[pl.BlockSpec(memory_space=pl.ANY)],
        scratch=[pltpu.SemaphoreType.DMA((3, 2))],
    )
    got = [swap(piece, "vir", k) for k, piece in zip((1, 2, 3), mine)]
    got = call(pack_metric, shape_of(3, part, 2 * rows), *got)
    by_x, by_y = swap(got, "occ", 2), swap(got, "occ", 4)
    halves = call(cut_metric, [shape_of(3, part, rows)] * 2, by_x, by_y)
    via_x, via_y = swap(halves[0], "occ", 2), swap(halves[1], "occ", 4)
    plane = [got, by_x, by_y, via_x, via_y]
    other = [swap(p, "occ", 1) for p in plane]
    half = pltpu.VMEM((3, rows, rows), BF16)
    whole = shape_of(aux, aux)
    return call(place_metric, whole, metric, *plane, *other, scratch=[half] * 2)


def row_chunks(rows, body, step=512):
    step = step if rows % step == 0 else rows
    for start in range(0, rows, step):
        body(slice(start, start + step))


def fit_rows(square, *refs):
    raws, out = refs[:-1], refs[-1]
    raw = jnp.concatenate([r[: square.shape[0], :] for r in raws], axis=1)

    def body(rows):
        out[rows, :] = dots(square[rows, :], raw, 1, 0).astype(BF16)

    row_chunks(square.shape[0], body)


def fit(square, *raws):
    aux = square.shape[0]
    unit = sum(raw.shape[1] for raw in raws)
    return call(fit_rows, shape_of(aux, unit), square, *raws, flops=2 * aux * aux * unit)


def energy_rows(occ_a, occ_o, occ_b, vir_a, vir_b, vir_n, left, right, *near):
    layer, me = lax.axis_index("vir"), lax.axis_index("occ")
    unit = vir_b.shape[1]
    for u, occ in enumerate((occ_a, occ_a, occ_o, occ_o)):
        row = vir_a[at((layer ^ (u % 2)) * unit, unit)].reshape(1, unit)
        left[u : u + 1, :] = occ[0] - row
    column = lambda vir: jnp.broadcast_to(occ_b[beta_of(me)] - vir, (128, unit)).T
    right[...] = column(vir_b[...])
    far = energy_of(vir_n[vir_n.shape[0] - TAIL :, :], unit)
    half = unit // 2
    for i, out in enumerate(near):
        out[...] = column(far)[i * half : (i + 1) * half]


def tile_rows(a0, a1, o0, o1, beta, left, right, mine, other, gamma, flip):
    alphas = (a0, a1, o0, o1)
    amp = [mine.at[0], mine.at[1], other.at[0], other.at[1]]
    flip[...] = beta[...].T
    column = right[:, :1]
    for u, alpha in enumerate(alphas):
        pair = dots(flip[...], alpha[...], 1, 0)
        amp[u][...] = (pair / (left[u : u + 1, :] + column)).astype(BF16)

    def body(rows):
        total = dots(a0[rows, :], amp[0][...], 1, 1)
        for u in (1, 2, 3):
            total = total + dots(alphas[u][rows, :], amp[u][...], 1, 1)
        gamma[rows, :] = total.astype(gamma.dtype)

    row_chunks(beta.shape[0], body)


def tile(alphas, beta, left, right, dtype):
    aux, width = beta.shape
    unit = alphas[0].shape[1]
    return call(
        tile_rows,
        [shape_of(2, width, unit)] * 2 + [shape_of(aux, width, dtype=dtype)],
        *alphas,
        beta,
        left,
        right,
        scratch=[pltpu.VMEM((width, aux), BF16)],
        flops=16 * aux * unit * width,
    )


def early_rows(*refs):
    betas, amps, out = refs[:4], refs[4:8], refs[8]
    unit = amps[0].shape[2]

    def body(rows):
        for u in (0, 1):
            total = dots(betas[0][rows, :], amps[0][u], 1, 0)
            for beta, amp in zip(betas[1:], amps[1:]):
                total = total + dots(beta[rows, :], amp[u], 1, 0)
            out[rows, u * unit : (u + 1) * unit] = total

    row_chunks(out.shape[0], body)


def mix_rows(early, beta_mine, beta_other, amp_mine, amp_other, own, near_zero, near_one, *outs):
    unit = amp_mine.shape[2]
    half = unit // 2
    odd = lax.axis_index("occ") % 2 == 1
    send2, send3, send4, keep2, keep3, keep4 = outs

    def body(rows):
        alpha = []
        for u in (0, 1):
            total = early[rows, u * unit : (u + 1) * unit]
            total = total + dots(beta_mine[rows, :], amp_mine[u], 1, 0)
            alpha.append(total + dots(beta_other[rows, :], amp_other[u], 1, 0))
        here, there = alpha[0], alpha[1].astype(BF16)
        beta, far = own[rows, :], near_one[rows, :]
        pick = lambda a, b: jnp.where(odd, a, b)
        send2[rows, :] = pick(there[:, :half], far)
        send3[rows, :] = there[:, half:]
        send4[rows, :half] = pick(near_zero[rows, :], there[:, :half])
        send4[rows, half:] = pick(far, there[:, half:])
        keep2[rows, :] = pick(here[:, :half], beta[:, half:])
        keep3[rows, :] = here[:, half:]
        keep4[rows, :] = pick(beta, here)

    row_chunks(early.shape[0], body, 256)


def sum_one(own_gamma, got, out):
    out[...] = (own_gamma[:, : out.shape[1]] + got[...].astype(F32)).astype(BF16)


def sum_keep(keep, got, out):
    out[...] = (keep[...] + got[...].astype(F32)).astype(BF16)


def last_rows(*refs):
    keep, got, move_a, move_b, move_c, alpha, beta, hold_a, hold_b, sems = refs
    odd = lax.axis_index("occ") % 2 == 1
    aux, half = move_a.shape
    step = aux // sems.shape[1]
    copies = []
    for i, start in enumerate(range(0, aux, step)):
        rows = slice(start, start + step)
        final = (keep[rows, :] + got[rows, :].astype(F32)).astype(BF16)
        low, high = final[:, :half], final[:, half:]
        hold_a[rows, :half] = jnp.where(odd, move_b[rows, :], low)
        hold_a[rows, half:] = jnp.where(odd, move_c[rows, :], high)
        hold_b[rows, :half] = jnp.where(odd, low, move_a[rows, :])
        hold_b[rows, half:] = jnp.where(odd, high, move_b[rows, :])
        for j, (hold, out) in enumerate(((hold_a, alpha), (hold_b, beta))):
            copy = pltpu.make_async_copy(hold.at[rows, :], out.at[rows, :], sems.at[j, i])
            copy.start()
            copies.append(copy)
    for copy in copies:
        copy.wait()


def last(*arrays):
    aux, half = arrays[-1].shape
    parts = 3
    anywhere = pl.BlockSpec(memory_space=pl.ANY)
    return pl.pallas_call(
        last_rows,
        out_shape=[shape_of(aux, 2 * half)] * 2,
        in_specs=[VMEM] * len(arrays),
        out_specs=[anywhere] * 2,
        scratch_shapes=[pltpu.VMEM((aux, 2 * half), BF16)] * 2
        + [pltpu.SemaphoreType.DMA((2, parts))],
        compiler_params=pltpu.CompilerParams(vmem_limit_bytes=8 << 20),
    )(*arrays)


def ring(ints_alpha, ints_beta, metric, e_occ_alpha, e_occ_beta, e_vir_alpha, e_vir_beta):
    aux = metric.shape[1]
    unit = e_vir_beta.shape[0]
    half = unit // 2
    blocks, layers = lax.axis_size("occ"), lax.axis_size("vir")
    assert layers == 4 and e_occ_alpha.shape[0] == 1

    square = whole_metric(metric)
    raw_beta = regroup(ints_beta, beta_of, 2, e_vir_beta[None])
    (raw_alpha,) = regroup(ints_alpha, alpha_of, 1)

    occ_mine = lax.ppermute(e_occ_alpha, "occ", [(alpha_of(d), d) for d in range(blocks)])
    occ_other = swap(occ_mine, "occ", 1)
    near_beta = []
    for raw in raw_beta:
        near_beta.append(swap(raw, "vir", 3))
    near_alpha = swap(raw_alpha, "vir", 1)

    left, right, right_zero, right_one = call(
        energy_rows,
        [shape_of(4, unit, dtype=F32)] + [shape_of(n, 128, dtype=F32) for n in (unit, half, half)],
        occ_mine,
        occ_other,
        e_occ_beta,
        e_vir_alpha,
        e_vir_beta[None],
        near_beta[0],
        specs=[SMEM] * 3 + [VMEM] * 3,
    )

    a0 = fit(square, raw_alpha)
    o0 = swap(a0, "occ", 1)
    b0 = fit(square, *raw_beta)
    a1 = fit(square, near_alpha)
    o1 = swap(a1, "occ", 1)
    alphas = (a0, a1, o0, o1)

    def both(array):
        return array, swap(array, "occ", 1)

    def tiles(beta, column, dtype):
        mine, other, gamma = tile(alphas, beta, left, column, dtype)
        return (mine, both(other)[1]), gamma

    b0, b0_other = both(b0)
    b1, b1_other = both(fit(square, near_beta[0]))
    amp_own, gamma_own = tiles(b0, right, F32)
    amp_zero, gamma_zero = tiles(b1, right_zero, BF16)

    def back(send, odd, even):
        pairs = [
            (d * layers + v, d * layers + (v ^ step))
            for d in range(blocks)
            for v in range(layers)
            for step in [odd if d % 2 else even]
            if step
        ]
        return lax.ppermute(send, ("occ", "vir"), pairs)

    got_one = back(gamma_zero, 0, 3)
    b2, b2_other = both(fit(square, near_beta[1]))
    amp_one, gamma_one = tiles(b2, right_one, BF16)
    betas, amps = (b0, b0_other, b1, b1_other), (*amp_own, *amp_zero)
    pair = shape_of(aux, 2 * unit, dtype=F32)
    early = call(early_rows, pair, *betas, *amps, flops=12 * aux * unit * unit)
    thin, thin32 = shape_of(aux, half), shape_of(aux, half, dtype=F32)
    send2, send3, send4, keep2, keep3, keep4 = call(
        mix_rows,
        [thin, thin, shape_of(aux, unit), thin32, thin32, shape_of(aux, unit, dtype=F32)],
        early,
        b2,
        b2_other,
        *amp_one,
        gamma_own,
        gamma_zero,
        gamma_one,
        flops=4 * aux * unit * unit,
    )
    got_two = back(send2, 1, 3)
    got_three = back(send3, 1, 0)
    got_four = back(send4, 3, 1)

    def move(value, cores):
        pairs = [(d, d ^ 2) for d in range(blocks) if d % 2 in cores]
        return lax.ppermute(value, "occ", pairs)

    first = call(sum_one, thin, gamma_own, got_one)
    second = call(sum_keep, thin, keep2, got_two)
    third = call(sum_keep, thin, keep3, got_three)
    moves = move(first, (0,)), move(second, (0, 1)), move(third, (1,))
    out_alpha, out_beta = last(keep4, got_four, *moves)
    return out_alpha.reshape(aux, 1, unit), out_beta.reshape(aux, 1, unit)


def solution(mesh):
    in_specs = (
        P("occ", None, "vir"),
        P("occ", None, "vir"),
        P("vir", None),
        P("occ"),
        P(),
        P(),
        P("vir"),
    )
    out_specs = (P(None, "occ", "vir"), P(None, "occ", "vir"))

    return jax.shard_map(ring, mesh=mesh, in_specs=in_specs, out_specs=out_specs, check_vma=False)
```

```python
import jax
import jax.numpy as jnp
from jax import lax
from jax.experimental import pallas as pl
from jax.experimental.pallas import tpu as pltpu
from jax.sharding import PartitionSpec as P

BF16, F32 = jnp.bfloat16, jnp.float32
TAIL = 16
VMEM = pl.BlockSpec(memory_space=pltpu.VMEM)
SMEM = pl.BlockSpec(memory_space=pltpu.SMEM)


def swap(value, axis, mask):
    pairs = [(source, source ^ mask) for source in range(lax.axis_size(axis))]
    return lax.ppermute(value, axis, pairs)


def alpha_of(device):
    return device ^ (2 * (device & 1))


def beta_of(device):
    return device ^ (2 * (1 - (device & 1)))


def shape_of(*dims, dtype=BF16):
    return jax.ShapeDtypeStruct(dims, dtype)


def call(kernel, shapes, *args, scratch=(), flops=0, specs=None):
    return pl.pallas_call(
        kernel,
        out_shape=shapes,
        in_specs=specs or [VMEM] * len(args),
        out_specs=jax.tree.map(lambda _: VMEM, shapes),
        scratch_shapes=scratch,
        cost_estimate=pl.CostEstimate(
            flops=flops, bytes_accessed=1 << 20, transcendentals=0
        ),
        compiler_params=pltpu.CompilerParams(vmem_limit_bytes=16 << 20),
    )(*args)


def dots(a, b, da, db):
    return lax.dot_general(a, b, (((da,), (db,)), ((), ())), preferred_element_type=F32)


def at(start, size):
    return pl.ds(pl.multiple_of(start, size), size)


def split_rows(index_of, chips, source, *refs):
    outs, table = refs[:-1], refs[-1]
    rows, blocks, cols = source.shape
    step = 16
    wide = step * blocks
    to = lax.broadcasted_iota(jnp.int32, (wide, wide), 0)
    by = lax.broadcasted_iota(jnp.int32, (wide, wide), 1)
    pick = jnp.where(by == (to % step) * blocks + to // step, 1.0, 0.0).astype(BF16)
    for q in range(0, rows, step):
        tile = dots(pick, source[q : q + step].reshape(wide, cols), 1, 0).astype(BF16)
        for d in range(blocks):
            table[d, q : q + step, :] = tile[d * step : (d + 1) * step]
    chip = lax.axis_index("occ") // 2
    for m in range(chips):
        for c in (0, 1):
            outs[m][c] = table[index_of(2 * (chip ^ m) + c)]


def give_rows(*refs):
    held, out = refs[:-1], refs[-1]
    core = lax.axis_index("occ") % 2
    for m, ref in enumerate(held):
        out[m] = ref[1 - core]


def energy_tail(value, width):
    parts = []
    for _ in range(3):
        parts.append(value.astype(BF16).astype(F32))
        value = value - parts[-1]
    lines = [p[:, k : k + width] for p in parts for k in range(0, value.shape[1], width)]
    row = lax.broadcasted_iota(jnp.int32, (TAIL, width), 0)
    tail = jnp.zeros((TAIL, width), F32)
    for i, line in enumerate(lines):
        tail = jnp.where(row == i, jnp.broadcast_to(line, (TAIL, width)), tail)
    return tail.astype(BF16)


def energy_of(tail, unit):
    value = tail.astype(F32)
    step = unit // tail.shape[1]
    line = lambda i: value[i : i + 1] + value[i + step : i + step + 1] + value[i + 2 * step : i + 2 * step + 1]
    return jnp.concatenate([line(i) for i in range(step)], axis=1)


def tail_rows(energy, out):
    out[...] = energy_tail(energy[...], out.shape[1])


def place_rows(chips, extra, *refs):
    held, take, outs = refs[:chips], refs[chips], refs[chips + 1 + extra :]
    rows = take.shape[1]
    me = lax.axis_index("occ")
    chip, core = me // 2, me % 2
    for m in range(chips):
        start = 2 * (chip ^ m) * rows
        for i, out in enumerate(outs):
            cols = slice(i * out.shape[1], (i + 1) * out.shape[1])
            out[at(start + core * rows, rows), :] = held[m][core, :, cols]
            out[at(start + (1 - core) * rows, rows), :] = take[m, :, cols]
    if extra:
        out = outs[0]
        out[2 * chips * rows :, :] = energy_tail(refs[chips + 1][...], out.shape[1])


def regroup(ints, index_of, parts, *extra):
    blocks = lax.axis_size("occ")
    chips = blocks // 2
    rows, _, cols = ints.shape
    if chips > 4:
        table = ints.transpose(1, 0, 2)
        table = jnp.stack([table[index_of(d)] for d in range(blocks)])
        got = lax.all_to_all(table, "occ", split_axis=0, concat_axis=0, tiled=True)
        got = jnp.split(got.reshape(blocks * rows, cols), parts, axis=1)
        for energy in extra:
            tail = call(tail_rows, shape_of(TAIL, cols // parts), energy)
            got[0] = jnp.concatenate([got[0], tail], axis=0)
        return got
    held = [*call(
        lambda *refs: split_rows(index_of, chips, *refs),
        [shape_of(2, rows, cols)] * chips,
        ints,
        scratch=[pltpu.VMEM((blocks, rows, cols), BF16)],
    )]
    for m in range(1, chips):
        held[m] = swap(held[m], "occ", 2 * m)
    give = call(give_rows, shape_of(chips, rows, cols), *held)
    take = swap(give, "occ", 1)
    place = lambda *refs: place_rows(chips, len(extra), *refs)
    tails = [TAIL * len(extra)] + [0] * (parts - 1)
    shapes = [shape_of(blocks * rows + tail, cols // parts) for tail in tails]
    return call(place, shapes, *held, take, *extra)


def halves_metric(metric):
    rows = metric.shape[0]
    half = rows // 2
    core, layer = lax.axis_index("occ") % 2, lax.axis_index("vir")
    mine = lax.dynamic_slice_in_dim(metric, core * half, half, 0)
    got = jnp.stack([swap(mine, "vir", k) for k in (1, 2, 3)])
    other = swap(got, "occ", 1)
    lo, hi = jnp.where(core == 0, got, other), jnp.where(core == 0, other, got)
    rest = jnp.concatenate([lo, hi], axis=1)
    pieces = [metric, rest[0], rest[1], rest[2]]
    return jnp.concatenate([lax.select_n(layer ^ k, *pieces) for k in range(4)], axis=0)


def near_of(k):
    return k - 1 if k > 1 else 3


def cut_own(metric, *refs):
    outs, sems = refs[:-1], refs[-1]
    part, wide = outs[0].shape[0], outs[0].shape[1] // 2
    layer = lax.axis_index("vir")
    rows = at(lax.axis_index("occ") * part, part)
    copies = []
    for k, out in zip((1, 2, 3), outs):
        for i, block in enumerate((layer, layer ^ k ^ near_of(k))):
            source = metric.at[rows, at(block * wide, wide)]
            target = out.at[:, i * wide : (i + 1) * wide]
            copies.append(pltpu.make_async_copy(source, target, sems.at[k - 1, i]))
            copies[-1].start()
    for copy in copies:
        copy.wait()


def pack_metric(*refs):
    for k, ref in enumerate(refs[:-1]):
        refs[-1][k] = ref[...]


def cut_metric(by_x, by_y, via_x, via_y):
    half = via_x.shape[2]
    via_x[...] = by_y[:, :, :half]
    via_y[...] = by_x[:, :, half:]


def place_metric(own, *refs):
    refs, out, same, cross = refs[:-3], *refs[-3:]
    mine, other = refs[: len(refs) // 2], refs[len(refs) // 2 :]
    rows = own.shape[0]
    part = mine[0].shape[1]
    me, layer = lax.axis_index("occ"), lax.axis_index("vir")
    chip, core = me // 2, me % 2
    for k in (0, 1, 2):
        for c, held in ((core, mine), (1 - core, other)):
            for m in range(4):
                here = at((2 * (chip ^ m) + c) * part, part)
                same[k, here, :] = held[m][k, :, :rows]
                cross[k, here, :] = held[4 if m == 3 else m][k, :, -rows:]
    block = lambda u: at(u * rows, rows)
    out[block(layer), :] = own[...]
    for k in (1, 2, 3):
        there, third = layer ^ k, layer ^ near_of(k)
        out[block(there), block(there)] = same[k - 1]
        out[block(there), block(third)] = cross[k - 1]
        out[block(third), block(there)] = cross[k - 1].T
        out[block(there), block(layer)] = own[:, block(there)].T


def whole_metric(metric):
    rows, aux = metric.shape
    blocks = lax.axis_size("occ")
    if blocks != 8 or rows % (16 * blocks) or rows % 128 or aux != 4 * rows:
        return halves_metric(metric)
    part = rows // blocks
    mine = call(
        cut_own,
        [shape_of(part, 2 * rows)] * 3,
        metric,
        specs=[pl.BlockSpec(memory_space=pl.ANY)],
        scratch=[pltpu.SemaphoreType.DMA((3, 2))],
    )
    got = [swap(piece, "vir", k) for k, piece in zip((1, 2, 3), mine)]
    got = call(pack_metric, shape_of(3, part, 2 * rows), *got)
    by_x, by_y = swap(got, "occ", 2), swap(got, "occ", 4)
    halves = call(cut_metric, [shape_of(3, part, rows)] * 2, by_x, by_y)
    via_x, via_y = swap(halves[0], "occ", 2), swap(halves[1], "occ", 4)
    plane = [got, by_x, by_y, via_x, via_y]
    other = [swap(p, "occ", 1) for p in plane]
    half = pltpu.VMEM((3, rows, rows), BF16)
    whole = shape_of(aux, aux)
    return call(place_metric, whole, metric, *plane, *other, scratch=[half] * 2)


def row_chunks(rows, body, step=512):
    step = step if rows % step == 0 else rows
    for start in range(0, rows, step):
        body(slice(start, start + step))


def fit_rows(square, *refs):
    raws, out = refs[:-1], refs[-1]
    raw = jnp.concatenate([r[: square.shape[0], :] for r in raws], axis=1)

    def body(rows):
        out[rows, :] = dots(square[rows, :], raw, 1, 0).astype(BF16)

    row_chunks(square.shape[0], body)


def fit(square, *raws):
    aux = square.shape[0]
    unit = sum(raw.shape[1] for raw in raws)
    return call(fit_rows, shape_of(aux, unit), square, *raws, flops=2 * aux * aux * unit)


def energy_rows(occ_a, occ_o, occ_b, vir_a, vir_b, vir_n, left, right, *near):
    layer, me = lax.axis_index("vir"), lax.axis_index("occ")
    unit = vir_b.shape[1]
    for u, occ in enumerate((occ_a, occ_a, occ_o, occ_o)):
        row = vir_a[at((layer ^ (u % 2)) * unit, unit)].reshape(1, unit)
        left[u : u + 1, :] = occ[0] - row
    column = lambda vir: jnp.broadcast_to(occ_b[beta_of(me)] - vir, (128, unit)).T
    right[...] = column(vir_b[...])
    far = energy_of(vir_n[vir_n.shape[0] - TAIL :, :], unit)
    half = unit // 2
    for i, out in enumerate(near):
        out[...] = column(far)[i * half : (i + 1) * half]


def tile_rows(a0, a1, o0, o1, beta, left, right, mine, other, gamma, flip):
    alphas = (a0, a1, o0, o1)
    amp = [mine.at[0], mine.at[1], other.at[0], other.at[1]]
    flip[...] = beta[...].T
    column = right[:, :1]
    for u, alpha in enumerate(alphas):
        pair = dots(flip[...], alpha[...], 1, 0)
        amp[u][...] = (pair / (left[u : u + 1, :] + column)).astype(BF16)

    def body(rows):
        total = dots(a0[rows, :], amp[0][...], 1, 1)
        for u in (1, 2, 3):
            total = total + dots(alphas[u][rows, :], amp[u][...], 1, 1)
        gamma[rows, :] = total.astype(gamma.dtype)

    row_chunks(beta.shape[0], body)


def tile(alphas, beta, left, right, dtype):
    aux, width = beta.shape
    unit = alphas[0].shape[1]
    return call(
        tile_rows,
        [shape_of(2, width, unit)] * 2 + [shape_of(aux, width, dtype=dtype)],
        *alphas,
        beta,
        left,
        right,
        scratch=[pltpu.VMEM((width, aux), BF16)],
        flops=16 * aux * unit * width,
    )


def early_rows(*refs):
    betas, amps, out = refs[:4], refs[4:8], refs[8]
    unit = amps[0].shape[2]

    def body(rows):
        for u in (0, 1):
            total = dots(betas[0][rows, :], amps[0][u], 1, 0)
            for beta, amp in zip(betas[1:], amps[1:]):
                total = total + dots(beta[rows, :], amp[u], 1, 0)
            out[rows, u * unit : (u + 1) * unit] = total

    row_chunks(out.shape[0], body)


def mix_rows(early, beta_mine, beta_other, amp_mine, amp_other, own, near_one, *outs):
    unit = amp_mine.shape[2]
    half = unit // 2
    odd = lax.axis_index("occ") % 2 == 1
    send2, send3, send4, keep2, keep3, keep4 = outs

    def body(rows):
        alpha = []
        for u in (0, 1):
            total = early[rows, u * unit : (u + 1) * unit]
            total = total + dots(beta_mine[rows, :], amp_mine[u], 1, 0)
            alpha.append(total + dots(beta_other[rows, :], amp_other[u], 1, 0))
        here, there = alpha[0], alpha[1].astype(BF16)
        beta, far = own[rows, :], near_one[rows, :]
        pick = lambda a, b: jnp.where(odd, a, b)
        send2[rows, :] = pick(there[:, :half], far)
        send3[rows, :] = there[:, half:]
        send4[rows, :] = there
        keep2[rows, :] = pick(here[:, :half], beta[:, half:])
        keep3[rows, :] = here[:, half:]
        keep4[rows, :] = pick(beta, here)

    row_chunks(early.shape[0], body, 256)


def sum_one(own_gamma, got, out):
    out[...] = (own_gamma[:, : out.shape[1]] + got[...].astype(F32)).astype(BF16)


def sum_keep(keep, got, out):
    out[...] = (keep[...] + got[...].astype(F32)).astype(BF16)


def last_rows(*refs):
    keep, got, one, six, four, move_a, move_b, move_c = refs[:8]
    alpha, beta, hold_a, hold_b, sems = refs[8:]
    odd = lax.axis_index("occ") % 2 == 1
    aux, half = move_a.shape
    step = aux // sems.shape[1]
    copies = []
    for i, start in enumerate(range(0, aux, step)):
        rows = slice(start, start + step)
        wide = got[rows, :].astype(F32)
        zero = one[rows, :].astype(F32) + six[rows, :].astype(F32)
        low = keep[rows, :half] + jnp.where(odd, zero, wide[:, :half])
        high = keep[rows, half:] + jnp.where(odd, four[rows, :].astype(F32), wide[:, half:])
        low, high = low.astype(BF16), high.astype(BF16)
        hold_a[rows, :half] = jnp.where(odd, move_b[rows, :], low)
        hold_a[rows, half:] = jnp.where(odd, move_c[rows, :], high)
        hold_b[rows, :half] = jnp.where(odd, low, move_a[rows, :])
        hold_b[rows, half:] = jnp.where(odd, high, move_b[rows, :])
        for j, (hold, out) in enumerate(((hold_a, alpha), (hold_b, beta))):
            copy = pltpu.make_async_copy(hold.at[rows, :], out.at[rows, :], sems.at[j, i])
            copy.start()
            copies.append(copy)
    for copy in copies:
        copy.wait()


def last(*arrays):
    aux, half = arrays[-1].shape
    parts = 3
    anywhere = pl.BlockSpec(memory_space=pl.ANY)
    return pl.pallas_call(
        last_rows,
        out_shape=[shape_of(aux, 2 * half)] * 2,
        in_specs=[VMEM] * len(arrays),
        out_specs=[anywhere] * 2,
        scratch_shapes=[pltpu.VMEM((aux, 2 * half), BF16)] * 2
        + [pltpu.SemaphoreType.DMA((2, parts))],
        compiler_params=pltpu.CompilerParams(vmem_limit_bytes=8 << 20),
    )(*arrays)


def ring(ints_alpha, ints_beta, metric, e_occ_alpha, e_occ_beta, e_vir_alpha, e_vir_beta):
    aux = metric.shape[1]
    unit = e_vir_beta.shape[0]
    half = unit // 2
    blocks, layers = lax.axis_size("occ"), lax.axis_size("vir")
    assert layers == 4 and e_occ_alpha.shape[0] == 1

    square = whole_metric(metric)
    raw_beta = regroup(ints_beta, beta_of, 2, e_vir_beta[None])
    (raw_alpha,) = regroup(ints_alpha, alpha_of, 1)

    occ_mine = lax.ppermute(e_occ_alpha, "occ", [(alpha_of(d), d) for d in range(blocks)])
    occ_other = swap(occ_mine, "occ", 1)
    near_beta = []
    for raw in raw_beta:
        near_beta.append(swap(raw, "vir", 3))
    near_alpha = swap(raw_alpha, "vir", 1)

    left, right, right_zero, right_one = call(
        energy_rows,
        [shape_of(4, unit, dtype=F32)] + [shape_of(n, 128, dtype=F32) for n in (unit, half, half)],
        occ_mine,
        occ_other,
        e_occ_beta,
        e_vir_alpha,
        e_vir_beta[None],
        near_beta[0],
        specs=[SMEM] * 3 + [VMEM] * 3,
    )

    a0 = fit(square, raw_alpha)
    o0 = swap(a0, "occ", 1)
    b0 = fit(square, *raw_beta)
    a1 = fit(square, near_alpha)
    o1 = swap(a1, "occ", 1)
    alphas = (a0, a1, o0, o1)

    def both(array):
        return array, swap(array, "occ", 1)

    def tiles(beta, column, dtype):
        mine, other, gamma = tile(alphas, beta, left, column, dtype)
        return (mine, both(other)[1]), gamma

    b0, b0_other = both(b0)
    b1, b1_other = both(fit(square, near_beta[0]))
    amp_own, gamma_own = tiles(b0, right, F32)
    amp_zero, gamma_zero = tiles(b1, right_zero, BF16)

    def back(send, step_of):
        pairs = [
            (d * layers + v, d * layers + (v ^ step))
            for d in range(blocks)
            for v in range(layers)
            for step in [step_of(d % 2, v in (0, layers - 1))]
            if step
        ]
        return lax.ppermute(send, ("occ", "vir"), pairs)

    got_one = back(gamma_zero, lambda odd, outer: 3 if outer or not odd else 0)
    b2, b2_other = both(fit(square, near_beta[1]))
    amp_one, gamma_one = tiles(b2, right_one, BF16)
    betas, amps = (b0, b0_other, b1, b1_other), (*amp_own, *amp_zero)
    pair = shape_of(aux, 2 * unit, dtype=F32)
    early = call(early_rows, pair, *betas, *amps, flops=12 * aux * unit * unit)
    thin, thin32 = shape_of(aux, half), shape_of(aux, half, dtype=F32)
    send2, send3, send4, keep2, keep3, keep4 = call(
        mix_rows,
        [thin, thin, shape_of(aux, unit), thin32, thin32, shape_of(aux, unit, dtype=F32)],
        early,
        b2,
        b2_other,
        *amp_one,
        gamma_own,
        gamma_one,
        flops=4 * aux * unit * unit,
    )
    got_two = back(send2, lambda odd, outer: 1 if odd else 3)
    got_three = back(send3, lambda odd, outer: 1 if odd else 0)
    got_four = back(gamma_one, lambda odd, outer: 3 if odd else 0)
    got_five = back(send4, lambda odd, outer: 0 if odd else 1)
    got_six = back(gamma_zero, lambda odd, outer: 3 if odd and not outer else 0)

    def move(value, cores):
        pairs = [(d, d ^ 2) for d in range(blocks) if d % 2 in cores]
        return lax.ppermute(value, "occ", pairs)

    first = call(sum_one, thin, gamma_own, got_one)
    second = call(sum_keep, thin, keep2, got_two)
    third = call(sum_keep, thin, keep3, got_three)
    moves = move(first, (0,)), move(second, (0, 1)), move(third, (1,))
    out_alpha, out_beta = last(keep4, got_five, got_one, got_six, got_four, *moves)
    return out_alpha.reshape(aux, 1, unit), out_beta.reshape(aux, 1, unit)


def solution(mesh):
    in_specs = (
        P("occ", None, "vir"),
        P("occ", None, "vir"),
        P("vir", None),
        P("occ"),
        P(),
        P(),
        P("vir"),
    )
    out_specs = (P(None, "occ", "vir"), P(None, "occ", "vir"))

    return jax.shard_map(ring, mesh=mesh, in_specs=in_specs, out_specs=out_specs, check_vma=False)
```

```python
import jax
import jax.numpy as jnp
from jax import lax
from jax.experimental import pallas as pl
from jax.experimental.pallas import tpu as pltpu
from jax.sharding import PartitionSpec as P

BF16, F32 = jnp.bfloat16, jnp.float32
TAIL = 16
VMEM = pl.BlockSpec(memory_space=pltpu.VMEM)
SMEM = pl.BlockSpec(memory_space=pltpu.SMEM)


def swap(value, axis, mask):
    pairs = [(source, source ^ mask) for source in range(lax.axis_size(axis))]
    return lax.ppermute(value, axis, pairs)


def alpha_of(device):
    return device ^ (2 * (device & 1))


def beta_of(device):
    return device ^ (2 * (1 - (device & 1)))


def shape_of(*dims, dtype=BF16):
    return jax.ShapeDtypeStruct(dims, dtype)


def call(kernel, shapes, *args, scratch=(), flops=0, specs=None):
    return pl.pallas_call(
        kernel,
        out_shape=shapes,
        in_specs=specs or [VMEM] * len(args),
        out_specs=jax.tree.map(lambda _: VMEM, shapes),
        scratch_shapes=scratch,
        cost_estimate=pl.CostEstimate(
            flops=flops, bytes_accessed=1 << 20, transcendentals=0
        ),
        compiler_params=pltpu.CompilerParams(vmem_limit_bytes=16 << 20),
    )(*args)


def dots(a, b, da, db):
    return lax.dot_general(a, b, (((da,), (db,)), ((), ())), preferred_element_type=F32)


def at(start, size):
    return pl.ds(pl.multiple_of(start, size), size)


def split_rows(index_of, chips, source, *refs):
    outs, table = refs[:-1], refs[-1]
    rows, blocks, cols = source.shape
    step = 16
    wide = step * blocks
    to = lax.broadcasted_iota(jnp.int32, (wide, wide), 0)
    by = lax.broadcasted_iota(jnp.int32, (wide, wide), 1)
    pick = jnp.where(by == (to % step) * blocks + to // step, 1.0, 0.0).astype(BF16)
    for q in range(0, rows, step):
        tile = dots(pick, source[q : q + step].reshape(wide, cols), 1, 0).astype(BF16)
        for d in range(blocks):
            table[d, q : q + step, :] = tile[d * step : (d + 1) * step]
    chip = lax.axis_index("occ") // 2
    for m in range(chips):
        for c in (0, 1):
            outs[m][c] = table[index_of(2 * (chip ^ m) + c)]


def give_rows(*refs):
    held, out = refs[:-1], refs[-1]
    core = lax.axis_index("occ") % 2
    for m, ref in enumerate(held):
        out[m] = ref[1 - core]


def energy_tail(value, width):
    parts = []
    for _ in range(3):
        parts.append(value.astype(BF16).astype(F32))
        value = value - parts[-1]
    lines = [p[:, k : k + width] for p in parts for k in range(0, value.shape[1], width)]
    row = lax.broadcasted_iota(jnp.int32, (TAIL, width), 0)
    tail = jnp.zeros((TAIL, width), F32)
    for i, line in enumerate(lines):
        tail = jnp.where(row == i, jnp.broadcast_to(line, (TAIL, width)), tail)
    return tail.astype(BF16)


def energy_of(tail, unit):
    value = tail.astype(F32)
    step = unit // tail.shape[1]
    line = lambda i: value[i : i + 1] + value[i + step : i + step + 1] + value[i + 2 * step : i + 2 * step + 1]
    return jnp.concatenate([line(i) for i in range(step)], axis=1)


def tail_rows(energy, out):
    out[...] = energy_tail(energy[...], out.shape[1])


def place_rows(chips, extra, *refs):
    held, take, outs = refs[:chips], refs[chips], refs[chips + 1 + extra :]
    rows = take.shape[1]
    me = lax.axis_index("occ")
    chip, core = me // 2, me % 2
    for m in range(chips):
        start = 2 * (chip ^ m) * rows
        for i, out in enumerate(outs):
            cols = slice(i * out.shape[1], (i + 1) * out.shape[1])
            out[at(start + core * rows, rows), :] = held[m][core, :, cols]
            out[at(start + (1 - core) * rows, rows), :] = take[m, :, cols]
    if extra:
        out = outs[0]
        out[2 * chips * rows :, :] = energy_tail(refs[chips + 1][...], out.shape[1])


def regroup(ints, index_of, parts, *extra):
    blocks = lax.axis_size("occ")
    chips = blocks // 2
    rows, _, cols = ints.shape
    if chips > 4:
        table = ints.transpose(1, 0, 2)
        table = jnp.stack([table[index_of(d)] for d in range(blocks)])
        got = lax.all_to_all(table, "occ", split_axis=0, concat_axis=0, tiled=True)
        got = jnp.split(got.reshape(blocks * rows, cols), parts, axis=1)
        for energy in extra:
            tail = call(tail_rows, shape_of(TAIL, cols // parts), energy)
            got[0] = jnp.concatenate([got[0], tail], axis=0)
        return got
    held = [*call(
        lambda *refs: split_rows(index_of, chips, *refs),
        [shape_of(2, rows, cols)] * chips,
        ints,
        scratch=[pltpu.VMEM((blocks, rows, cols), BF16)],
    )]
    for m in range(1, chips):
        held[m] = swap(held[m], "occ", 2 * m)
    give = call(give_rows, shape_of(chips, rows, cols), *held)
    take = swap(give, "occ", 1)
    place = lambda *refs: place_rows(chips, len(extra), *refs)
    tails = [TAIL * len(extra)] + [0] * (parts - 1)
    shapes = [shape_of(blocks * rows + tail, cols // parts) for tail in tails]
    return call(place, shapes, *held, take, *extra)


def halves_metric(metric):
    rows = metric.shape[0]
    half = rows // 2
    core, layer = lax.axis_index("occ") % 2, lax.axis_index("vir")
    mine = lax.dynamic_slice_in_dim(metric, core * half, half, 0)
    got = jnp.stack([swap(mine, "vir", k) for k in (1, 2, 3)])
    other = swap(got, "occ", 1)
    lo, hi = jnp.where(core == 0, got, other), jnp.where(core == 0, other, got)
    rest = jnp.concatenate([lo, hi], axis=1)
    pieces = [metric, rest[0], rest[1], rest[2]]
    return jnp.concatenate([lax.select_n(layer ^ k, *pieces) for k in range(4)], axis=0)


def near_of(k):
    return k - 1 if k > 1 else 3


def cut_own(metric, *refs):
    outs, sems = refs[:-1], refs[-1]
    part, wide = outs[0].shape[0], outs[0].shape[1] // 2
    layer = lax.axis_index("vir")
    rows = at(lax.axis_index("occ") * part, part)
    copies = []
    for k, out in zip((1, 2, 3), outs):
        for i, block in enumerate((layer, layer ^ k ^ near_of(k))):
            source = metric.at[rows, at(block * wide, wide)]
            target = out.at[:, i * wide : (i + 1) * wide]
            copies.append(pltpu.make_async_copy(source, target, sems.at[k - 1, i]))
            copies[-1].start()
    for copy in copies:
        copy.wait()


def pack_metric(*refs):
    for k, ref in enumerate(refs[:-1]):
        refs[-1][k] = ref[...]


def cut_metric(by_x, by_y, via_x, via_y):
    half = via_x.shape[2]
    via_x[...] = by_y[:, :, :half]
    via_y[...] = by_x[:, :, half:]


def place_metric(own, *refs):
    refs, out, same, cross = refs[:-3], *refs[-3:]
    mine, other = refs[: len(refs) // 2], refs[len(refs) // 2 :]
    rows = own.shape[0]
    part = mine[0].shape[1]
    me, layer = lax.axis_index("occ"), lax.axis_index("vir")
    chip, core = me // 2, me % 2
    for k in (0, 1, 2):
        for c, held in ((core, mine), (1 - core, other)):
            for m in range(4):
                here = at((2 * (chip ^ m) + c) * part, part)
                same[k, here, :] = held[m][k, :, :rows]
                cross[k, here, :] = held[4 if m == 3 else m][k, :, -rows:]
    block = lambda u: at(u * rows, rows)
    out[block(layer), :] = own[...]
    for k in (1, 2, 3):
        there, third = layer ^ k, layer ^ near_of(k)
        out[block(there), block(there)] = same[k - 1]
        out[block(there), block(third)] = cross[k - 1]
        out[block(third), block(there)] = cross[k - 1].T
        out[block(there), block(layer)] = own[:, block(there)].T


def whole_metric(metric):
    rows, aux = metric.shape
    blocks = lax.axis_size("occ")
    if blocks != 8 or rows % (16 * blocks) or rows % 128 or aux != 4 * rows:
        return halves_metric(metric)
    part = rows // blocks
    mine = call(
        cut_own,
        [shape_of(part, 2 * rows)] * 3,
        metric,
        specs=[pl.BlockSpec(memory_space=pl.ANY)],
        scratch=[pltpu.SemaphoreType.DMA((3, 2))],
    )
    got = [swap(piece, "vir", k) for k, piece in zip((1, 2, 3), mine)]
    got = call(pack_metric, shape_of(3, part, 2 * rows), *got)
    by_x, by_y = swap(got, "occ", 2), swap(got, "occ", 4)
    halves = call(cut_metric, [shape_of(3, part, rows)] * 2, by_x, by_y)
    via_x, via_y = swap(halves[0], "occ", 2), swap(halves[1], "occ", 4)
    plane = [got, by_x, by_y, via_x, via_y]
    other = [swap(p, "occ", 1) for p in plane]
    half = pltpu.VMEM((3, rows, rows), BF16)
    whole = shape_of(aux, aux)
    return call(place_metric, whole, metric, *plane, *other, scratch=[half] * 2)


def row_chunks(rows, body, step=512):
    step = step if rows % step == 0 else rows
    for start in range(0, rows, step):
        body(slice(start, start + step))


def fit_rows(square, *refs):
    raws, out = refs[:-1], refs[-1]
    raw = jnp.concatenate([r[: square.shape[0], :] for r in raws], axis=1)

    def body(rows):
        out[rows, :] = dots(square[rows, :], raw, 1, 0).astype(BF16)

    row_chunks(square.shape[0], body)


def fit(square, *raws):
    aux = square.shape[0]
    unit = sum(raw.shape[1] for raw in raws)
    return call(fit_rows, shape_of(aux, unit), square, *raws, flops=2 * aux * aux * unit)


def energy_rows(occ_a, occ_o, occ_b, vir_a, vir_b, vir_n, left, right, *near):
    layer, me = lax.axis_index("vir"), lax.axis_index("occ")
    unit = vir_b.shape[1]
    for u, occ in enumerate((occ_a, occ_a, occ_o, occ_o)):
        row = vir_a[at((layer ^ (u % 2)) * unit, unit)].reshape(1, unit)
        left[u : u + 1, :] = occ[0] - row
    column = lambda vir: jnp.broadcast_to(occ_b[beta_of(me)] - vir, (128, unit)).T
    right[...] = column(vir_b[...])
    far = energy_of(vir_n[vir_n.shape[0] - TAIL :, :], unit)
    half = unit // 2
    for i, out in enumerate(near):
        out[...] = column(far)[i * half : (i + 1) * half]


def tile_rows(a0, a1, o0, o1, beta, left, right, mine, other, gamma, flip):
    alphas = (a0, a1, o0, o1)
    amp = [mine.at[0], mine.at[1], other.at[0], other.at[1]]
    flip[...] = beta[...].T
    column = right[:, :1]
    for u, alpha in enumerate(alphas):
        pair = dots(flip[...], alpha[...], 1, 0)
        amp[u][...] = (pair / (left[u : u + 1, :] + column)).astype(BF16)

    def body(rows):
        total = dots(a0[rows, :], amp[0][...], 1, 1)
        for u in (1, 2, 3):
            total = total + dots(alphas[u][rows, :], amp[u][...], 1, 1)
        gamma[rows, :] = total.astype(gamma.dtype)

    row_chunks(beta.shape[0], body)


def tile(alphas, beta, left, right, dtype):
    aux, width = beta.shape
    unit = alphas[0].shape[1]
    return call(
        tile_rows,
        [shape_of(2, width, unit)] * 2 + [shape_of(aux, width, dtype=dtype)],
        *alphas,
        beta,
        left,
        right,
        scratch=[pltpu.VMEM((width, aux), BF16)],
        flops=16 * aux * unit * width,
    )


def alpha_rows(u, rows, betas, amps, total=None):
    for beta, amp in zip(betas, amps):
        term = dots(beta[rows, :], amp[u], 1, 0)
        total = term if total is None else total + term
    return total


def early_rows(*refs):
    betas, amps, out = refs[:4], refs[4:8], refs[8]

    def body(rows):
        out[rows, :] = alpha_rows(1, rows, betas, amps)

    row_chunks(out.shape[0], body)


def mix_rows(early, near_one, *refs):
    betas, amps = refs[:2], refs[2:4]
    send2, send3, send4 = refs[4:]
    half = near_one.shape[1]
    odd = lax.axis_index("occ") % 2 == 1

    def body(rows):
        there = alpha_rows(1, rows, betas, amps, early[rows, :]).astype(BF16)
        send2[rows, :] = jnp.where(odd, there[:, :half], near_one[rows, :])
        send3[rows, :] = there[:, half:]
        send4[rows, :] = there

    row_chunks(early.shape[0], body)


def keep_rows(own, *refs):
    betas, amps = refs[:6], refs[6:12]
    keep2, keep3, keep4 = refs[12:]
    half = keep2.shape[1]
    odd = lax.axis_index("occ") % 2 == 1

    def body(rows):
        here, beta = alpha_rows(0, rows, betas, amps), own[rows, :]
        keep2[rows, :] = jnp.where(odd, here[:, :half], beta[:, half:])
        keep3[rows, :] = here[:, half:]
        keep4[rows, :] = jnp.where(odd, beta, here)

    row_chunks(own.shape[0], body)


def sum_one(own_gamma, got, out):
    out[...] = (own_gamma[:, : out.shape[1]] + got[...].astype(F32)).astype(BF16)


def sum_keep(keep, got, out):
    out[...] = (keep[...] + got[...].astype(F32)).astype(BF16)


def last_rows(*refs):
    keep, got, one, six, four, move_a, move_b, move_c = refs[:8]
    alpha, beta, hold_a, hold_b, sems = refs[8:]
    odd = lax.axis_index("occ") % 2 == 1
    aux, half = move_a.shape
    step = aux // sems.shape[1]
    copies = []
    for i, start in enumerate(range(0, aux, step)):
        rows = slice(start, start + step)
        wide = got[rows, :].astype(F32)
        zero = one[rows, :].astype(F32) + six[rows, :].astype(F32)
        low = keep[rows, :half] + jnp.where(odd, zero, wide[:, :half])
        high = keep[rows, half:] + jnp.where(odd, four[rows, :].astype(F32), wide[:, half:])
        low, high = low.astype(BF16), high.astype(BF16)
        hold_a[rows, :half] = jnp.where(odd, move_b[rows, :], low)
        hold_a[rows, half:] = jnp.where(odd, move_c[rows, :], high)
        hold_b[rows, :half] = jnp.where(odd, low, move_a[rows, :])
        hold_b[rows, half:] = jnp.where(odd, high, move_b[rows, :])
        for j, (hold, out) in enumerate(((hold_a, alpha), (hold_b, beta))):
            copy = pltpu.make_async_copy(hold.at[rows, :], out.at[rows, :], sems.at[j, i])
            copy.start()
            copies.append(copy)
    for copy in copies:
        copy.wait()


def last(*arrays):
    aux, half = arrays[-1].shape
    parts = 3
    anywhere = pl.BlockSpec(memory_space=pl.ANY)
    return pl.pallas_call(
        last_rows,
        out_shape=[shape_of(aux, 2 * half)] * 2,
        in_specs=[VMEM] * len(arrays),
        out_specs=[anywhere] * 2,
        scratch_shapes=[pltpu.VMEM((aux, 2 * half), BF16)] * 2
        + [pltpu.SemaphoreType.DMA((2, parts))],
        compiler_params=pltpu.CompilerParams(vmem_limit_bytes=8 << 20),
    )(*arrays)


def ring(ints_alpha, ints_beta, metric, e_occ_alpha, e_occ_beta, e_vir_alpha, e_vir_beta):
    aux = metric.shape[1]
    unit = e_vir_beta.shape[0]
    half = unit // 2
    blocks, layers = lax.axis_size("occ"), lax.axis_size("vir")
    assert layers == 4 and e_occ_alpha.shape[0] == 1

    square = whole_metric(metric)
    raw_beta = regroup(ints_beta, beta_of, 2, e_vir_beta[None])
    (raw_alpha,) = regroup(ints_alpha, alpha_of, 1)

    occ_mine = lax.ppermute(e_occ_alpha, "occ", [(alpha_of(d), d) for d in range(blocks)])
    occ_other = swap(occ_mine, "occ", 1)
    near_beta = []
    for raw in raw_beta:
        near_beta.append(swap(raw, "vir", 3))
    near_alpha = swap(raw_alpha, "vir", 1)

    left, right, right_zero, right_one = call(
        energy_rows,
        [shape_of(4, unit, dtype=F32)] + [shape_of(n, 128, dtype=F32) for n in (unit, half, half)],
        occ_mine,
        occ_other,
        e_occ_beta,
        e_vir_alpha,
        e_vir_beta[None],
        near_beta[0],
        specs=[SMEM] * 3 + [VMEM] * 3,
    )

    a0 = fit(square, raw_alpha)
    o0 = swap(a0, "occ", 1)
    b0 = fit(square, *raw_beta)
    a1 = fit(square, near_alpha)
    o1 = swap(a1, "occ", 1)
    alphas = (a0, a1, o0, o1)

    def both(array):
        return array, swap(array, "occ", 1)

    def tiles(beta, column, dtype):
        mine, other, gamma = tile(alphas, beta, left, column, dtype)
        return (mine, both(other)[1]), gamma

    b0, b0_other = both(b0)
    b1, b1_other = both(fit(square, near_beta[0]))
    amp_own, gamma_own = tiles(b0, right, F32)
    amp_zero, gamma_zero = tiles(b1, right_zero, BF16)

    def back(send, step_of):
        pairs = [
            (d * layers + v, d * layers + (v ^ step))
            for d in range(blocks)
            for v in range(layers)
            for step in [step_of(d % 2, v in (0, layers - 1))]
            if step
        ]
        return lax.ppermute(send, ("occ", "vir"), pairs)

    got_one = back(gamma_zero, lambda odd, outer: 3 if outer or not odd else 0)
    b2, b2_other = both(fit(square, near_beta[1]))
    amp_one, gamma_one = tiles(b2, right_one, BF16)
    betas, amps = (b0, b0_other, b1, b1_other), (*amp_own, *amp_zero)
    work = 2 * aux * unit * unit
    thin, wide = shape_of(aux, half), shape_of(aux, unit)
    thin32, wide32 = shape_of(aux, half, dtype=F32), shape_of(aux, unit, dtype=F32)
    early = call(early_rows, wide32, *betas, *amps, flops=3 * work)
    ends = (b2, b2_other, *amp_one)
    sends = call(mix_rows, [thin, thin, wide], early, gamma_one, *ends, flops=work)
    send2, send3, send4 = sends
    keeps = [thin32, thin32, wide32]
    arrays = (*betas, *ends[:2], *amps, *ends[2:])
    keep2, keep3, keep4 = call(keep_rows, keeps, gamma_own, *arrays, flops=4 * work)
    got_two = back(send2, lambda odd, outer: 1 if odd else 3)
    got_three = back(send3, lambda odd, outer: 1 if odd else 0)
    got_four = back(gamma_one, lambda odd, outer: 3 if odd else 0)
    got_five = back(send4, lambda odd, outer: 0 if odd else 1)
    got_six = back(gamma_zero, lambda odd, outer: 3 if odd and not outer else 0)

    def move(value, cores):
        pairs = [(d, d ^ 2) for d in range(blocks) if d % 2 in cores]
        return lax.ppermute(value, "occ", pairs)

    first = call(sum_one, thin, gamma_own, got_one)
    second = call(sum_keep, thin, keep2, got_two)
    third = call(sum_keep, thin, keep3, got_three)
    moves = move(first, (0,)), move(second, (0, 1)), move(third, (1,))
    out_alpha, out_beta = last(keep4, got_five, got_one, got_six, got_four, *moves)
    return out_alpha.reshape(aux, 1, unit), out_beta.reshape(aux, 1, unit)


def solution(mesh):
    in_specs = (
        P("occ", None, "vir"),
        P("occ", None, "vir"),
        P("vir", None),
        P("occ"),
        P(),
        P(),
        P("vir"),
    )
    out_specs = (P(None, "occ", "vir"), P(None, "occ", "vir"))

    return jax.shard_map(ring, mesh=mesh, in_specs=in_specs, out_specs=out_specs, check_vma=False)
```
